128 devices in a mesh: lat: 4 (over z), lon: 32 (over y, x, core).
Axes of the slice: x: 4, y: 4, z: 4, core: 2. Of those that a mesh axis runs over, the one named last changes fastest.
Arguments:
- mesh_latent: bfloat16 [32, 256, 512], P('lat', 'lon'), may hold values from -6 to 6
- grid_cotangent: bfloat16 [131072, 512], P(('lat', 'lon')), may hold values from -6 to 6
- w_source: bfloat16 [512, 512], replicated, may hold values from -0.25 to 0.25
- w_target: bfloat16 [512, 512], replicated, may hold values from -0.25 to 0.25
- w_node: bfloat16 [512, 512], replicated, may hold values from -0.25 to 0.25
- w_coarse: bfloat16 [512, 512], replicated, may hold values from -0.25 to 0.25
- w_decode: bfloat16 [512, 512], replicated, may hold values from -0.25 to 0.25
- neighbour_codes: int32 [6, 32, 256], P(None, 'lat', 'lon'), may hold values from 0 to 8, as said below
- coarse_ids: int32 [32, 256, 1], P('lat', 'lon'), may hold values from 0 to 641
- edge_source: int32 [393216], P(('lat', 'lon')), may hold values from 0 to 63
- edge_target: int32 [393216], P(('lat', 'lon')), may hold values from 0 to 1023
- edge_owner: int32 [3072, 1], P(('lat', 'lon')), may hold values from 0 to 31, as said below
Outputs:
- mesh_out: bfloat16 [32, 256, 512], P('lat', 'lon')
- grid_out: bfloat16 [131072, 512], P(('lat', 'lon'))
- clipped: float32 [5, 262144], P(None, ('lat', 'lon'))
The draws below stay inside these ranges and needn't reach their ends.
Inputs may be any that keep to these rules, and one draw needn't show every extreme that they name: `neighbour_codes`: code c names the row offset c // 3 - 1 and the column offset c % 3 - 1 and is never 4; the six codes of one node differ. `coarse_ids`: every coarse node has at least one mesh node. `edge_owner`: the owner of a block held by the device at longitude index b is b, or b - 1 or b + 1 on the periodic cycle of longitude indices. Among the 24 blocks of one device at most 3 name b - 1 and at most 3 name b + 1; in every draw some device receives 3 blocks from each of its two neighbours.
All inputs are finite; a program needn't handle non-finite values.
Results may differ from the reference program's by a relative error of at most 0.008.
Values may be sent and summed in bfloat16 or wider, within the bound.
No kernel may reach another device: no remote copies, remote signals or barrier semaphores. Data moves between devices by JAX's collectives and lax.ppermute only.
A program may use at most 64 MiB of HBM per device.

```python
import jax
import jax.numpy as jnp
from jax import lax

D = 512
ROWS_DEV = 8
COLS_DEV = 8
GRID_DEV = 1024
BLOCK = 128
COARSE = 642
BLOCKS_DEV = 24
CAP = 3
MESH_ROWS = 32
MESH_COLS = 256
GRID = 131072
EDGES = 393216
N_LAT = 4
N_LON = 32
DEVICES = 128


def draw_neighbour_codes(key, part):
    scores = jax.random.randint(key, (N_LAT * ROWS_DEV, N_LON * COLS_DEV, 8), 0, 1 << 20) * 8 + jnp.arange(8, dtype=jnp.int32)
    order = jnp.argsort(scores, axis=-1, stable=True)[..., :6]
    codes = order + (order >= 4).astype(jnp.int32)
    return jnp.transpose(codes, (2, 0, 1)).astype(jnp.int32)


def draw_edge_owner(key, part):
    devices = N_LAT * N_LON
    base = jax.random.fold_in(key, 7)
    key_counts, key_star, key_order = jax.random.split(base, 3)
    counts = jax.random.randint(key_counts, (devices, 2), 0, CAP + 1).astype(jnp.int32)
    star = jax.random.randint(key_star, (), 0, devices).astype(jnp.int32)
    star_lat = star // N_LON
    star_lon = star % N_LON
    sender_left = star_lat * N_LON + (star_lon + N_LON - 1) % N_LON
    sender_right = star_lat * N_LON + (star_lon + 1) % N_LON
    dev_ids = jnp.arange(devices, dtype=jnp.int32)
    to_left = jnp.where(dev_ids == sender_right, CAP, counts[:, 0])
    to_right = jnp.where(dev_ids == sender_left, CAP, counts[:, 1])
    scores = jax.random.randint(key_order, (devices, BLOCKS_DEV), 0, 1 << 20) * BLOCKS_DEV + jnp.arange(BLOCKS_DEV, dtype=jnp.int32)[None]
    order = jnp.argsort(scores, axis=1, stable=True)
    ranks = jnp.argsort(order, axis=1, stable=True).astype(jnp.int32)
    offset = jnp.where(ranks < to_left[:, None], -1, jnp.where(ranks < (to_left + to_right)[:, None], 1, 0))
    lon_ids = dev_ids % N_LON
    owner = (lon_ids[:, None] + offset + N_LON) % N_LON
    return owner.reshape(devices * BLOCKS_DEV, 1).astype(jnp.int32)


def with_ends(array, rng, low, high):
    longest = array.shape.index(max(array.shape))
    spots = []
    for shift in (0, 1):
        where = [jax.random.randint(jax.random.fold_in(rng, axis), (), 0, length) for axis, length in enumerate(array.shape)]
        where[longest] = (where[longest] + shift) % array.shape[longest]
        spots.append(tuple(where))
    return array.at[spots[0]].set(low).at[spots[1]].set(high)


def block_levels(key, extent, shards, low, top_value):
    gain, own = 1.0, jax.random.fold_in(key, 6)
    for axis_at, parts in shards:
        draws = jnp.exp(jax.random.uniform(jax.random.fold_in(own, axis_at), (parts,), jnp.float32, low / len(shards), top_value / len(shards)))
        gain = gain * jnp.repeat(draws, extent[axis_at] // parts).reshape([-1 if axis == axis_at else 1 for axis in range(len(extent))])
    return gain


def different_ones(stream_key, rows, number_of, top, lift):
    sequence = jax.random.permutation(jax.random.fold_in(stream_key, 1), number_of)
    pull = sequence
    for power in range(3):
        pull = pull * pull // number_of
    pull = pull * lift // number_of
    lots = jax.random.randint(jax.random.fold_in(stream_key, 2), (rows, number_of), 0, 4096) + pull
    fixed_rows = jax.random.permutation(jax.random.fold_in(stream_key, 3), rows)[jnp.arange(number_of) % rows]
    lots = jnp.where(jnp.arange(rows)[:, None] == fixed_rows[None, :], 1 << 14, lots)
    merit = lots * number_of + jnp.arange(number_of)
    return lax.top_k(merit.astype(jnp.int32), top)[1].astype(jnp.int32)


def bell_draw(stream_key, dims, scale, reach, shards=(), held_as=jnp.bfloat16):
    entries = jax.random.normal(stream_key, dims, jnp.float32) * scale
    if len(shards) > 0:
        entries = block_levels(stream_key, dims, shards, -0.22, 0.18) * entries
    return jnp.clip(entries, min=-reach, max=reach).astype(held_as)


def setup_inputs(seed: int = 0) -> dict:
    arg_keys = jax.random.split(jax.random.key(seed), 13)
    return {
        "mesh_latent": bell_draw(arg_keys[0], (MESH_ROWS, MESH_COLS, D), 1.0, 6.0, ((0, 4), (1, 32))),
        "grid_cotangent": bell_draw(arg_keys[1], (GRID, D), 1.0, 6.0, ((0, 128),)),
        "w_source": bell_draw(arg_keys[2], (D, D), D ** -0.5, 0.25),
        "w_target": bell_draw(arg_keys[3], (D, D), D ** -0.5, 0.25),
        "w_node": bell_draw(arg_keys[4], (D, D), D ** -0.5, 0.25),
        "w_coarse": bell_draw(arg_keys[5], (D, D), D ** -0.5, 0.25),
        "w_decode": bell_draw(arg_keys[6], (D, D), D ** -0.5, 0.25),
        "neighbour_codes": draw_neighbour_codes(jax.random.fold_in(arg_keys[12], 71), 0),
        "coarse_ids": different_ones(arg_keys[8], MESH_ROWS * MESH_COLS, COARSE, 1, 12).reshape((MESH_ROWS, MESH_COLS, 1)),
        "edge_source": with_ends(jax.random.randint(arg_keys[9], (EDGES,), 0, ROWS_DEV * COLS_DEV), jax.random.fold_in(arg_keys[9], 1), 0, (ROWS_DEV * COLS_DEV) - 1).astype(jnp.int32),
        "edge_target": with_ends(jax.random.randint(arg_keys[10], (EDGES,), 0, GRID_DEV), jax.random.fold_in(arg_keys[10], 1), 0, GRID_DEV - 1).astype(jnp.int32),
        "edge_owner": draw_edge_owner(jax.random.fold_in(arg_keys[12], 71), 0),
    }


def silu_slope(value):
    sig = jax.nn.sigmoid(value)
    return sig * (1.0 + value * (1.0 - sig))

def reference(mesh_latent, grid_cotangent, w_source, w_target, w_node, w_coarse, w_decode, neighbour_codes, coarse_ids, edge_source, edge_target, edge_owner):
    height, breadth, width = mesh_latent.shape
    nodes = height * breadth
    wrapped = jnp.concatenate([mesh_latent[:, -1:], mesh_latent, mesh_latent[:, :1]], 1)
    padded = jnp.pad(wrapped, ((1, 1), (0, 0), (0, 0)))
    flat_pad = padded.reshape(-1, width)
    row_at = jnp.arange(height, dtype=jnp.int32)[None, :, None] + neighbour_codes // 3
    col_at = jnp.arange(breadth, dtype=jnp.int32)[None, None, :] + neighbour_codes % 3
    where_idx = (row_at * (breadth + 2) + col_at).reshape(-1).astype(jnp.int32)
    beside = jnp.take(flat_pad, where_idx, axis=0)
    latent = mesh_latent.reshape(nodes, width)
    toward = jnp.dot(latent, w_target, preferred_element_type=jnp.float32)
    edges_pre = jnp.dot(beside, w_source, preferred_element_type=jnp.float32).reshape(6, nodes, width) + toward[None]
    agg = lax.optimization_barrier(jnp.sum(jax.nn.silu(edges_pre), 0)).astype(jnp.bfloat16)
    onehot = (coarse_ids.reshape(nodes, 1) == jnp.arange(COARSE, dtype=jnp.int32)[None]).astype(jnp.bfloat16)
    pooled = jnp.dot(onehot.T, latent, preferred_element_type=jnp.float32)
    count = lax.optimization_barrier(jnp.sum(onehot.astype(jnp.float32), 0))
    coarse_in = (pooled * lax.rsqrt(count)[:, None]).astype(jnp.bfloat16)
    cpre = jnp.dot(coarse_in, w_coarse, preferred_element_type=jnp.float32)
    coarse_out = jax.nn.silu(cpre).astype(jnp.bfloat16)
    child = jnp.dot(onehot, coarse_out, preferred_element_type=jnp.float32)
    npre = jnp.dot(agg, w_node, preferred_element_type=jnp.float32) + child
    mesh_out = (latent.astype(jnp.float32) + jax.nn.silu(npre)).astype(jnp.bfloat16)
    per_dev = BLOCKS_DEV * BLOCK
    edge_ids = jnp.arange(EDGES, dtype=jnp.int32)
    device = edge_ids // per_dev
    lat_pos = device // N_LON
    lon_pos = device % N_LON
    owner = jnp.repeat(edge_owner[:, 0], BLOCK).astype(jnp.int32)
    src_row = lat_pos * ROWS_DEV + edge_source // COLS_DEV
    src_col = lon_pos * COLS_DEV + edge_source % COLS_DEV
    src_flat = (src_row * breadth + src_col).astype(jnp.int32)
    target = ((lat_pos * N_LON + owner) * GRID_DEV + edge_target).astype(jnp.int32)

    def decode_step(carry, pieces):
        grid_acc, grad_acc, source_acc = carry
        sources, targets = pieces
        gathered = jnp.take(mesh_out, sources, axis=0)
        pre = jnp.dot(gathered, w_decode, preferred_element_type=jnp.float32)
        message = jax.nn.silu(pre).astype(jnp.bfloat16)
        grid_acc = grid_acc.at[targets].add(message.astype(jnp.float32))
        edge_cot = jnp.take(grid_cotangent, targets, axis=0).astype(jnp.float32)
        d_pre = (edge_cot * silu_slope(pre)).astype(jnp.bfloat16)
        grad_acc = grad_acc + jnp.dot(gathered.T, d_pre, preferred_element_type=jnp.float32)
        source_acc = source_acc.at[sources].add(d_pre.astype(jnp.float32))
        return ((grid_acc, grad_acc, source_acc), None)
    start = (jnp.zeros((GRID, width), jnp.float32), jnp.zeros((width, width), jnp.float32), jnp.zeros((nodes, width), jnp.float32))
    pieces = (src_flat.reshape(DEVICES, per_dev), target.reshape(DEVICES, per_dev))
    (grid_acc, grad_decode, source_acc), _ = lax.scan(decode_step, start, pieces)
    grid_out = grid_acc.astype(jnp.bfloat16)
    per_source = source_acc.astype(jnp.bfloat16)
    d_out = jnp.dot(per_source, w_decode.T, preferred_element_type=jnp.float32)
    d_node = (d_out * silu_slope(npre)).astype(jnp.bfloat16)
    grad_node = jnp.dot(agg.T, d_node, preferred_element_type=jnp.float32)
    d_coarse = jnp.dot(onehot.T, d_node, preferred_element_type=jnp.float32)
    grad_coarse = jnp.dot(coarse_in.astype(jnp.float32).T, d_coarse * silu_slope(cpre), precision=lax.Precision.HIGHEST)
    d_agg = jnp.dot(d_node, w_node.T, preferred_element_type=jnp.float32)
    d_edges = (d_agg[None] * silu_slope(edges_pre)).astype(jnp.bfloat16)
    grad_source = jnp.dot(beside.T, d_edges.reshape(6 * nodes, width), preferred_element_type=jnp.float32)
    d_sum = lax.optimization_barrier(jnp.sum(d_edges.astype(jnp.float32), 0)).astype(jnp.bfloat16)
    grad_target = jnp.dot(latent.T, d_sum, preferred_element_type=jnp.float32)
    grads = jnp.stack([grad_source, grad_target, grad_node, grad_coarse, grad_decode])
    norm = jnp.sqrt(jnp.sum(grads * grads))
    clipped = (grads / (norm + 1e-06)).reshape(5, width * width)
    return (mesh_out.reshape(height, breadth, width), grid_out, clipped)
```

```python
import jax
import jax.numpy as jnp
from jax import lax
from jax.experimental import pallas as pl
from jax.experimental.pallas import tpu as pltpu
from jax.sharding import Mesh
from jax.sharding import PartitionSpec as P

CAP = 3
CHIPS = ("z", "y", "x")
LON = ("y", "x", "c")
EVERY = ("z", "y", "x", "c")
BF = jnp.bfloat16
F32 = jnp.float32
I32 = jnp.int32
NODES = 64
D = 512
SLOTS = 8
TABLE = 128
N_CHIPS = 64
MSG = 1280


def dot(a, b):
    return jnp.dot(a, b, preferred_element_type=F32)


def dot_nt(a, b):
    return lax.dot_general(a, b, (((1,), (1,)), ((), ())), preferred_element_type=F32)


def dot_tn(a, b):
    return lax.dot_general(a, b, (((0,), (0,)), ((), ())), preferred_element_type=F32)


def iota(shape, dim):
    return lax.broadcasted_iota(I32, shape, dim)


def hot(mask):
    return jnp.where(mask, 1.0, 0.0).astype(BF)


def slope_of(value, sig):
    return sig * (1.0 + value * (1.0 - sig))


def column_of(small):
    rows = small.shape[0]
    count = rows * 8
    spread = dot(hot(iota((count, rows), 0) // 8 == iota((count, rows), 1)), small.astype(F32).astype(BF))
    keep = iota((count, 8), 0) % 8 == iota((count, 8), 1)
    return jnp.sum(jnp.where(keep, spread, 0.0), axis=1, keepdims=True)


def row_of(column):
    count = column.shape[0]
    eye = iota((count, count), 0) == iota((count, count), 1)
    return jnp.sum(jnp.where(eye, column, 0.0), axis=0, keepdims=True)


def id_columns(ids_ref, core):
    ids = ids_ref[...].reshape(8, 8)
    half = ids >> 1
    chip = column_of(half & 63)
    slot = column_of(half >> 6)
    mine = column_of(ids & 1) == core.astype(F32)
    return chip, slot, mine


def pool_kernel(ids_ref, ids_other_ref, h_ref, h_other_ref, out_ref):
    core = lax.axis_index("c")
    a = id_columns(ids_ref, core)
    b = id_columns(ids_other_ref, core)
    chip, slot, mine = (jnp.concatenate([u, v], 0) for u, v in zip(a, [b[0], b[1], b[2]]))
    base = chip * SLOTS
    place = row_of(jnp.where(mine, base + slot, -1.0)).astype(I32)
    place_count = row_of(jnp.where(mine, base + 6.0, -1.0)).astype(I32)
    rows = iota((N_CHIPS * SLOTS, 2 * NODES), 0)
    which = hot(iota((2 * NODES, D), 1) == slot.astype(I32))
    both = jnp.concatenate([h_ref[...], h_other_ref[...]], 0)
    out_ref[...] = (dot(hot(rows == place), both) + dot(hot(rows == place_count), which)).astype(BF)


def coarse_kernel(got_ref, out_ref):
    total = jnp.sum(got_ref[...].astype(F32), axis=0)
    counts = jnp.broadcast_to(total[6:7, :], (SLOTS, D))
    keep = iota((SLOTS, D), 0) == iota((SLOTS, D), 1)
    count = jnp.sum(jnp.where(keep, counts, 0.0), axis=1, keepdims=True)
    scale = jnp.where(count > 0.5, lax.rsqrt(jnp.maximum(count, 1.0)), 0.0)
    out_ref[...] = jnp.broadcast_to((total * scale).astype(BF)[None], (N_CHIPS, SLOTS, D))


def select_kernel(ids_ref, ids_other_ref, got_ref, out_ref):
    core = lax.axis_index("c")
    a = id_columns(ids_ref, core)
    b = id_columns(ids_other_ref, core)
    chip, slot, mine = (jnp.concatenate([u, v], 0) for u, v in zip(a, b))
    place = jnp.where(mine, chip * SLOTS + slot, -1.0).astype(I32)
    chosen = hot(iota((2 * NODES, N_CHIPS * SLOTS), 1) == place)
    out_ref[...] = dot(chosen, got_ref[...]).astype(BF)


def halo_kernel(above_ref, h_ref, below_ref, block_ref, first_ref, last_ref):
    block = jnp.concatenate([above_ref[...], h_ref[...], below_ref[...]], 0)
    block_ref[...] = block
    at = iota((16, 80), 1)
    row = iota((16, 80), 0)
    first_ref[...] = dot(hot(at == row * 8), block).astype(BF)
    last_ref[...] = dot(hot(at == row * 8 + 7), block).astype(BF)


def lists_kernel(owner_ref, source_ref, target_ref, left_ref, right_ref, own_ref):
    lon = lax.axis_index(LON)
    lists = (left_ref, right_ref)
    for ref in lists:
        ref[...] = jnp.full(ref.shape, -1, I32)
    ranks = [jnp.int32(0), jnp.int32(0)]
    for b in range(source_ref.shape[0]):
        side = (owner_ref[b] - lon) & 31
        source = source_ref[b : b + 1, :]
        target = target_ref[b : b + 1, :]
        own_ref[b : b + 1, :] = jnp.where(side == 0, target, -1)
        for k, code in enumerate((31, 1)):
            here = side == code
            place = jnp.where(here, jnp.minimum(ranks[k], 6), 7)
            lists[k][pl.ds(place, 1), :] = source
            lists[k][pl.ds(place + 8, 1), :] = target
            ranks[k] = ranks[k] + here.astype(I32)


def counts_kernel(source_ref, target_ref, left_ref, right_ref, cot_ref, ct_ref, own_ref, to_left_ref, to_right_ref):
    grid_rows = cot_ref.shape[0]

    def counted(sources, targets):
        at = iota((grid_rows, 128), 0)
        node = iota((NODES, 128), 0)
        hit = jnp.concatenate([hot(at == t) for t in targets], 1)
        come = jnp.concatenate([hot(node == s) for s in sources], 1)
        return dot_nt(come, hit)

    blocks = source_ref.shape[0]
    step = 4
    total = jnp.zeros((NODES, grid_rows), F32)
    for b in range(0, blocks, step):
        total = total + counted(
            [source_ref[i : i + 1, :] for i in range(b, b + step)],
            [target_ref[i : i + 1, :] for i in range(b, b + step)],
        )
    sums = []
    for k, (ref, out) in enumerate(((None, own_ref), (left_ref, to_left_ref), (right_ref, to_right_ref))):
        if k:
            total = counted(
                [ref[i : i + 1, :] for i in range(CAP)],
                [ref[8 + i : 9 + i, :] for i in range(CAP)],
            )
        table = total.astype(BF)
        ct_ref[k * NODES : (k + 1) * NODES, :] = table
        out[...] = dot(table, cot_ref[...]).astype(out.dtype)


def shifted(value, side, core):
    wide = value.astype(F32)
    amount = 4 if side else D - 4
    moved = pltpu.roll(wide, amount, 1)
    lanes = iota(value.shape, 1)
    kept = ((lanes >> 2) & 1) == side
    picked = jnp.where(core == side, wide, moved)
    return jnp.where(kept, picked, 0.0).astype(BF)


def edges_kernel(
    codes_ref, codes_other_ref, table_ref, table_other_ref, ws_ref, wt_ref, wn_ref,
    hot_ref, slope_ref, agg_ref, aggw_ref,
):
    lanes = iota((6 * NODES, TABLE), 1)
    for k, (codes, table) in enumerate(((codes_ref, table_ref), (codes_other_ref, table_other_ref))):
        code = column_of(codes[...].reshape(48, 8)).astype(I32)
        node = iota((6 * NODES, 1), 0) % NODES
        down = (code * 11) >> 5
        row = node // 8 + down
        col = node % 8 + code - 3 * down
        place = jnp.where(col == 0, 80 + row, jnp.where(col == 9, 96 + row, row * 8 + col - 1))
        chosen = hot(lanes == place)
        hot_ref[k * 6 * NODES : (k + 1) * 6 * NODES, :] = chosen
        rows = jnp.concatenate([table[...], jnp.zeros((16, D), BF)], 0)
        beside = dot(chosen, rows).astype(BF)
        toward = dot(table[8:72, :], wt_ref[...])
        pre = dot(beside, ws_ref[...])
        agg = jnp.zeros((NODES, D), F32)
        for s in range(6):
            value = pre[s * NODES : (s + 1) * NODES, :] + toward
            sig = jax.nn.sigmoid(value)
            agg = agg + value * sig
            at = (k * 6 + s) * NODES
            slope_ref[at : at + NODES, :] = slope_of(value, sig)
        agg = agg.astype(BF)
        agg_ref[k * NODES : (k + 1) * NODES, :] = agg
        aggw_ref[k * NODES : (k + 1) * NODES, :] = dot(agg, wn_ref[...])


def main_kernel(
    cin_ref, cin_other_ref, table_ref, table_other_ref, hot_ref, slope_ref, agg_ref, aggw_ref,
    gs_ref, gs_other_ref, wc_ref, wd_ref, wn_ref,
    mesh_ref, message_ref, msg_ref,
):
    core = lax.axis_index("c")
    cin = jnp.concatenate(
        [
            cin_ref[:NODES, :].astype(F32) + cin_other_ref[NODES:, :].astype(F32),
            cin_ref[NODES:, :].astype(F32) + cin_other_ref[:NODES, :].astype(F32),
        ],
        0,
    ).astype(BF)
    h = jnp.concatenate([table_ref[8:72, :], table_other_ref[8:72, :]], 0)
    cpre = dot(cin, wc_ref[...])
    csig = jax.nn.sigmoid(cpre)
    npre = aggw_ref[...] + (cpre * csig).astype(BF).astype(F32)
    nsig = jax.nn.sigmoid(npre)
    mesh_out = (h.astype(F32) + npre * nsig).astype(BF)
    mesh_ref[...] = mesh_out[:NODES, :]
    pre = dot(mesh_out, wd_ref[...])
    sig = jax.nn.sigmoid(pre)
    message_ref[...] = (pre * sig).astype(BF)[:NODES, :]
    gs = jnp.concatenate([gs_ref[...], gs_other_ref[...]], 0)
    d_source = (gs * slope_of(pre, sig)).astype(BF)
    d_out = dot_nt(d_source, wd_ref[...])
    d_node = (d_out * slope_of(npre, nsig)).astype(BF)
    d_agg = dot_nt(d_node, wn_ref[...])
    d_coarse = (d_node.astype(F32) * slope_of(cpre, csig)).astype(BF)
    scattered, sums = [], []
    for k in range(2):
        d_edges = []
        part = d_agg[k * NODES : (k + 1) * NODES, :]
        d_sum = jnp.zeros((NODES, D), F32)
        for s in range(6):
            at = (k * 6 + s) * NODES
            d_edge = (part * slope_ref[at : at + NODES, :]).astype(BF)
            d_sum = d_sum + d_edge.astype(F32)
            d_edges.append(d_edge)
        sums.append(d_sum.astype(BF))
        at = k * 6 * NODES
        scattered.append(dot_tn(hot_ref[at : at + 6 * NODES, :], jnp.concatenate(d_edges, 0)).astype(BF))
    zeros = jnp.zeros((16, D), BF)
    tables = jnp.concatenate([table_ref[...], zeros, table_other_ref[...], zeros], 0)
    msg_ref[:, :D] = dot_tn(
        jnp.concatenate([shifted(tables, 0, core), shifted(h, 1, core)], 0),
        jnp.concatenate(scattered + sums, 0),
    ).astype(BF)
    msg_ref[:, D : 2 * D] = dot_tn(
        jnp.concatenate([shifted(agg_ref[...], 0, core), shifted(cin, 1, core)], 0),
        jnp.concatenate([d_node, d_coarse], 0),
    ).astype(BF)
    msg_ref[:, 2 * D :] = dot_tn(
        jnp.concatenate([shifted(mesh_out, 0, core), shifted(mesh_out, 1, core)], 0),
        jnp.concatenate([d_source[:, : D // 2], d_source[:, D // 2 :]], 0),
    ).astype(BF)


def grid_kernel(ct_ref, own_ref, left_ref, right_ref, out_ref):
    rows = jnp.concatenate([own_ref[...], left_ref[...], right_ref[...]], 0)
    out_ref[...] = dot_tn(ct_ref[...], rows).astype(BF)


def sum_kernel(got_ref, share_ref, square_ref):
    total = jnp.sum(got_ref[...].astype(F32), axis=0)
    share_ref[...] = total
    square = jnp.sum(jnp.sum(total * total, axis=0, keepdims=True), axis=1, keepdims=True)
    square_ref[...] = jnp.broadcast_to(square, square_ref.shape)


def clip_kernel(squares_ref, share_ref, out_ref):
    total = jnp.sum(squares_ref[...], axis=0, keepdims=True)
    norm = jnp.sqrt(jnp.max(total, axis=1, keepdims=True)) + 1e-06
    value = share_ref[...] / norm
    for m in range(5):
        for r in range(4):
            if m < 4:
                row = (m % 2) * 4 + r
                line = value[row : row + 1, (m // 2) * D : (m // 2 + 1) * D]
            else:
                line = jnp.concatenate(
                    [value[r : r + 1, 2 * D :], value[r + 4 : r + 5, 2 * D :]], 1
                )
            out_ref[m : m + 1, r * D : (r + 1) * D] = line


def call(kernel, outs, *args, smem=()):
    specs = [
        pl.BlockSpec(memory_space=pltpu.SMEM if i in smem else pltpu.VMEM) for i in range(len(args))
    ]
    shapes = [jax.ShapeDtypeStruct(s, d) for s, d in outs]
    out = pl.pallas_call(
        kernel,
        out_shape=shapes,
        in_specs=specs,
        out_specs=[pl.BlockSpec(memory_space=pltpu.VMEM) for _ in outs],
        name=kernel.__name__,
    )(*args)
    return out if len(outs) > 1 else out[0]


def local(
    mesh_latent, grid_cotangent, w_source, w_target, w_node, w_coarse, w_decode,
    neighbour_codes, coarse_ids, edge_source, edge_target, edge_owner,
):
    height, breadth, width = mesh_latent.shape
    nodes = height * breadth
    grid_rows = grid_cotangent.shape[0]
    blocks = edge_owner.shape[0]
    flip = [(0, 1), (1, 0)]
    plus = [(i, (i + 1) % 32) for i in range(32)]
    minus = [((i + 1) % 32, i) for i in range(32)]

    def other(value):
        return lax.ppermute(value, "c", flip)

    def to_right(value):
        return lax.ppermute(value, LON, plus)

    def to_left(value):
        return lax.ppermute(value, LON, minus)

    def swapped(value):
        return lax.all_to_all(value, CHIPS, split_axis=0, concat_axis=0, tiled=True)

    h = mesh_latent.reshape(nodes, width)
    ids = jnp.transpose(coarse_ids, (0, 2, 1))
    ids_other = other(ids)
    pooled = call(pool_kernel, [((N_CHIPS * SLOTS, D), BF)], ids, ids_other, h, other(h))
    pooled = swapped(pooled.reshape(N_CHIPS, SLOTS, D))
    coarse = call(coarse_kernel, [((N_CHIPS, SLOTS, D), BF)], pooled)
    coarse = swapped(coarse).reshape(N_CHIPS * SLOTS, D)
    cin = call(select_kernel, [((2 * NODES, D), BF)], ids, ids_other, coarse)
    cin_other = other(cin)

    above = lax.ppermute(mesh_latent[height - 1], "z", [(i, i + 1) for i in range(3)])
    below = lax.ppermute(mesh_latent[0], "z", [(i + 1, i) for i in range(3)])
    block, first, last = call(
        halo_kernel, [((80, D), BF), ((16, D), BF), ((16, D), BF)], above, h, below
    )
    table = jnp.concatenate([block, to_right(last), to_left(first)], 0)
    table_other = other(table)
    codes_other = other(neighbour_codes)

    source = edge_source.reshape(blocks, -1)
    target = edge_target.reshape(blocks, -1)
    list_left, list_right, own_target = call(
        lists_kernel,
        [((16, 128), I32), ((16, 128), I32), ((blocks, 128), I32)],
        edge_owner.reshape(blocks), source, target, smem=(0,),
    )
    ct, gs_own, gs_left, gs_right = call(
        counts_kernel,
        [((3 * NODES, grid_rows), BF), ((NODES, D), F32), ((NODES, D), BF), ((NODES, D), BF)],
        source, own_target, to_right(list_right), to_left(list_left), grid_cotangent,
    )
    gs = gs_own + to_left(gs_left).astype(F32) + to_right(gs_right).astype(F32)
    gs_other = other(gs)

    chosen, slopes, agg, aggw = call(
        edges_kernel,
        [((12 * NODES, TABLE), BF), ((12 * NODES, D), F32), ((2 * NODES, D), BF), ((2 * NODES, D), F32)],
        neighbour_codes, codes_other, table, table_other, w_source, w_target, w_node,
    )
    mesh_out, message, msg = call(
        main_kernel,
        [((NODES, D), BF), ((NODES, D), BF), ((N_CHIPS * 8, MSG), BF)],
        cin, cin_other, table, table_other, chosen, slopes, agg, aggw, gs, gs_other,
        w_coarse, w_decode, w_node,
    )
    arrived = swapped(msg.reshape(N_CHIPS, 8, MSG))
    grid_out = call(grid_kernel, [((grid_rows, D), BF)], ct, message, to_right(message), to_left(message))
    share, square = call(sum_kernel, [((8, MSG), F32), ((128, 128), F32)], arrived)
    squares = lax.all_to_all(
        square.reshape(128, 1, 128), EVERY, split_axis=0, concat_axis=0, tiled=True
    ).reshape(128, 128)
    clipped = call(clip_kernel, [((5, 4 * D), F32)], squares, share)
    return mesh_out.reshape(height, breadth, width), grid_out, clipped


def solution(mesh):
    split = Mesh(mesh.devices.reshape(4, 4, 4, 2), EVERY)
    return jax.shard_map(
        local,
        mesh=split,
        in_specs=(
            P("z", LON, None),
            P(EVERY, None),
            P(),
            P(),
            P(),
            P(),
            P(),
            P(None, "z", LON),
            P("z", LON, None),
            P(EVERY),
            P(EVERY),
            P(EVERY, None),
        ),
        out_specs=(P("z", LON, None), P(EVERY, None), P(None, EVERY)),
        check_vma=False,
    )
```

```python
import jax
import jax.numpy as jnp
from jax import lax
from jax.experimental import pallas as pl
from jax.experimental.pallas import tpu as pltpu
from jax.sharding import Mesh
from jax.sharding import PartitionSpec as P

CAP = 3
CHIPS = ("z", "y", "x")
LON = ("y", "x", "c")
EVERY = ("z", "y", "x", "c")
BF = jnp.bfloat16
F32 = jnp.float32
I32 = jnp.int32
NODES = 64
D = 512
SLOTS = 8
BLOCK_ROWS = 80
TABLE = 384
N_CHIPS = 64
MSG = 1280


def dot(a, b):
    return jnp.dot(a, b, preferred_element_type=F32)


def dot_nt(a, b):
    return lax.dot_general(a, b, (((1,), (1,)), ((), ())), preferred_element_type=F32)


def dot_tn(a, b):
    return lax.dot_general(a, b, (((0,), (0,)), ((), ())), preferred_element_type=F32)


def iota(shape, dim):
    return lax.broadcasted_iota(I32, shape, dim)


def hot(mask):
    return jnp.where(mask, 1.0, 0.0).astype(BF)


def slope_of(value, sig):
    return sig * (1.0 + value * (1.0 - sig))


def column_of(small):
    rows = small.shape[0]
    count = rows * 8
    spread = dot(hot(iota((count, rows), 0) // 8 == iota((count, rows), 1)), small.astype(F32).astype(BF))
    keep = iota((count, 8), 0) % 8 == iota((count, 8), 1)
    return jnp.sum(jnp.where(keep, spread, 0.0), axis=1, keepdims=True)


def row_of(column):
    count = column.shape[0]
    eye = iota((count, count), 0) == iota((count, count), 1)
    return jnp.sum(jnp.where(eye, column, 0.0), axis=0, keepdims=True)


def id_columns(ids_ref, core):
    ids = ids_ref[...].reshape(8, 8)
    half = ids >> 1
    chip = column_of(half & 63)
    slot = column_of(half >> 6)
    mine = column_of(ids & 1) == core.astype(F32)
    return chip, slot, mine


def pool_kernel(ids_ref, ids_other_ref, h_ref, h_other_ref, out_ref):
    core = lax.axis_index("c")
    a = id_columns(ids_ref, core)
    b = id_columns(ids_other_ref, core)
    chip, slot, mine = (jnp.concatenate([u, v], 0) for u, v in zip(a, [b[0], b[1], b[2]]))
    base = chip * SLOTS
    place = row_of(jnp.where(mine, base + slot, -1.0)).astype(I32)
    place_count = row_of(jnp.where(mine, base + 6.0, -1.0)).astype(I32)
    rows = iota((N_CHIPS * SLOTS, 2 * NODES), 0)
    which = hot(iota((2 * NODES, D), 1) == slot.astype(I32))
    both = jnp.concatenate([h_ref[...], h_other_ref[...]], 0)
    out_ref[...] = (dot(hot(rows == place), both) + dot(hot(rows == place_count), which)).astype(BF)


def coarse_kernel(got_ref, _done, out_ref):
    total = jnp.sum(got_ref[...].astype(F32), axis=0)
    counts = jnp.broadcast_to(total[6:7, :], (SLOTS, D))
    keep = iota((SLOTS, D), 0) == iota((SLOTS, D), 1)
    count = jnp.sum(jnp.where(keep, counts, 0.0), axis=1, keepdims=True)
    scale = jnp.where(count > 0.5, lax.rsqrt(jnp.maximum(count, 1.0)), 0.0)
    out_ref[...] = jnp.broadcast_to((total * scale).astype(BF)[None], (N_CHIPS, SLOTS, D))


def select_kernel(ids_ref, ids_other_ref, got_ref, _agg, _gs, out_ref):
    core = lax.axis_index("c")
    a = id_columns(ids_ref, core)
    b = id_columns(ids_other_ref, core)
    chip, slot, mine = (jnp.concatenate([u, v], 0) for u, v in zip(a, b))
    place = jnp.where(mine, chip * SLOTS + slot, -1.0).astype(I32)
    chosen = hot(iota((2 * NODES, N_CHIPS * SLOTS), 1) == place)
    out_ref[...] = dot(chosen, got_ref[...]).astype(BF)


def halo_kernel(above_ref, h_ref, below_ref, block_ref):
    block_ref[...] = jnp.concatenate([above_ref[...], h_ref[...], below_ref[...]], 0)


def lists_kernel(owner_ref, source_ref, target_ref, other_ref, far_ref, own_ref):
    lon = lax.axis_index(LON)
    code_other = jnp.where(lax.axis_index("c") == 0, 1, 31)
    lists = (other_ref, far_ref)
    for ref in lists:
        ref[...] = jnp.full(ref.shape, -1, I32)
    ranks = [jnp.int32(0), jnp.int32(0)]
    for b in range(source_ref.shape[0]):
        side = (owner_ref[b] - lon) & 31
        source = source_ref[b : b + 1, :]
        target = target_ref[b : b + 1, :]
        own_ref[b : b + 1, :] = jnp.where(side == 0, target, -1)
        for k, code in enumerate((code_other, 32 - code_other)):
            here = side == code
            place = jnp.where(here, jnp.minimum(ranks[k], 6), 7)
            lists[k][pl.ds(place, 1), :] = source
            lists[k][pl.ds(place + 8, 1), :] = target
            ranks[k] = ranks[k] + here.astype(I32)


def counts_kernel(source_ref, target_ref, other_ref, far_ref, cot_ref, ct_ref, own_ref, to_other_ref, to_far_ref, done_ref):
    done_ref[...] = jnp.zeros(done_ref.shape, F32)
    grid_rows = cot_ref.shape[0]

    def counted(sources, targets):
        at = iota((grid_rows, 128), 0)
        node = iota((NODES, 128), 0)
        hit = jnp.concatenate([hot(at == t) for t in targets], 1)
        come = jnp.concatenate([hot(node == s) for s in sources], 1)
        return dot_nt(come, hit)

    blocks = source_ref.shape[0]
    step = 4
    total = jnp.zeros((NODES, grid_rows), F32)
    for b in range(0, blocks, step):
        total = total + counted(
            [source_ref[i : i + 1, :] for i in range(b, b + step)],
            [target_ref[i : i + 1, :] for i in range(b, b + step)],
        )
    for k, (ref, out) in enumerate(((None, own_ref), (other_ref, to_other_ref), (far_ref, to_far_ref))):
        if k:
            total = counted(
                [ref[i : i + 1, :] for i in range(CAP)],
                [ref[8 + i : 9 + i, :] for i in range(CAP)],
            )
        table = total.astype(BF)
        ct_ref[k * NODES : (k + 1) * NODES, :] = table
        out[...] = dot(table, cot_ref[...]).astype(out.dtype)


def shifted(value, side, core):
    wide = value.astype(F32)
    amount = 4 if side else D - 4
    moved = pltpu.roll(wide, amount, 1)
    lanes = iota(value.shape, 1)
    kept = ((lanes >> 2) & 1) == side
    picked = jnp.where(core == side, wide, moved)
    return jnp.where(kept, picked, 0.0).astype(BF)


def whole_table(refs):
    blocks = [ref[...] for ref in refs]
    return jnp.concatenate([*blocks, jnp.zeros((TABLE - 4 * BLOCK_ROWS, D), BF)], 0)


def chosen_rows(codes_ref, k):
    toward_left = jnp.where(lax.axis_index("c") == 0, -1, 1)
    code = column_of(codes_ref[...].reshape(48, 8)).astype(I32)
    node = iota((6 * NODES, 1), 0) % NODES
    down = (code * 11) >> 5
    row = node // 8 + down
    col = node % 8 + code - 3 * down - 1
    step = jnp.where(col < 0, toward_left, jnp.where(col > 7, -toward_left, 0))
    place = (1 + k + step) * BLOCK_ROWS + row * 8 + (col & 7)
    return hot(iota((6 * NODES, TABLE), 1) == place)


def edges_kernel(
    codes_ref, codes_other_ref, far_ref, own_ref, other_ref, other_far_ref, ws_ref, wt_ref,
    slope_ref, agg_ref,
):
    table = whole_table((far_ref, own_ref, other_ref, other_far_ref))
    for k, (codes, own) in enumerate(((codes_ref, own_ref), (codes_other_ref, other_ref))):
        beside = dot(chosen_rows(codes, k), table).astype(BF)
        toward = dot(own[8:72, :], wt_ref[...])
        pre = dot(beside, ws_ref[...])
        agg = jnp.zeros((NODES, D), F32)
        for s in range(6):
            value = pre[s * NODES : (s + 1) * NODES, :] + toward
            sig = jax.nn.sigmoid(value)
            agg = agg + value * sig
            at = (k * 6 + s) * NODES
            slope_ref[at : at + NODES, :] = slope_of(value, sig).astype(BF)
        agg_ref[k * NODES : (k + 1) * NODES, :] = agg.astype(BF)


def main_kernel(
    cin_ref, cin_other_ref, codes_ref, codes_other_ref, far_ref, own_ref, other_ref, other_far_ref,
    slope_ref, agg_ref, gs_ref, gs_other_ref, wc_ref, wd_ref, wn_ref,
    mesh_ref, message_ref, msg_ref,
):
    core = lax.axis_index("c")
    chosen = jnp.concatenate([chosen_rows(codes_ref, 0), chosen_rows(codes_other_ref, 1)], 0)
    cin = jnp.concatenate(
        [
            cin_ref[:NODES, :].astype(F32) + cin_other_ref[NODES:, :].astype(F32),
            cin_ref[NODES:, :].astype(F32) + cin_other_ref[:NODES, :].astype(F32),
        ],
        0,
    ).astype(BF)
    h = jnp.concatenate([own_ref[8:72, :], other_ref[8:72, :]], 0)
    cpre = dot(cin, wc_ref[...])
    csig = jax.nn.sigmoid(cpre)
    npre = dot(agg_ref[...], wn_ref[...]) + (cpre * csig).astype(BF).astype(F32)
    nsig = jax.nn.sigmoid(npre)
    mesh_out = (h.astype(F32) + npre * nsig).astype(BF)
    mesh_ref[...] = mesh_out[:NODES, :]
    pre = dot(mesh_out, wd_ref[...])
    sig = jax.nn.sigmoid(pre)
    message_ref[...] = (pre * sig).astype(BF)[:NODES, :]
    gs = jnp.concatenate([gs_ref[...], gs_other_ref[...]], 0)
    d_source = (gs * slope_of(pre, sig)).astype(BF)
    d_out = dot_nt(d_source, wd_ref[...])
    d_node = (d_out * slope_of(npre, nsig)).astype(BF)
    d_agg = dot_nt(d_node, wn_ref[...])
    d_coarse = (d_node.astype(F32) * slope_of(cpre, csig)).astype(BF)
    d_edges, sums = [], []
    for k in range(2):
        part = d_agg[k * NODES : (k + 1) * NODES, :]
        d_sum = jnp.zeros((NODES, D), F32)
        for s in range(6):
            at = (k * 6 + s) * NODES
            d_edge = (part * slope_ref[at : at + NODES, :].astype(F32)).astype(BF)
            d_sum = d_sum + d_edge.astype(F32)
            d_edges.append(d_edge)
        sums.append(d_sum.astype(BF))
    scattered = dot_tn(chosen, jnp.concatenate(d_edges, 0)).astype(BF)
    table = whole_table((far_ref, own_ref, other_ref, other_far_ref))
    msg_ref[:, :D] = dot_tn(
        jnp.concatenate([shifted(table, 0, core), shifted(h, 1, core)], 0),
        jnp.concatenate([scattered, *sums], 0),
    ).astype(BF)
    msg_ref[:, D : 2 * D] = dot_tn(
        jnp.concatenate([shifted(agg_ref[...], 0, core), shifted(cin, 1, core)], 0),
        jnp.concatenate([d_node, d_coarse], 0),
    ).astype(BF)
    msg_ref[:, 2 * D :] = dot_tn(
        jnp.concatenate([shifted(mesh_out, 0, core), shifted(mesh_out, 1, core)], 0),
        jnp.concatenate([d_source[:, : D // 2], d_source[:, D // 2 :]], 0),
    ).astype(BF)


def grid_kernel(ct_ref, own_ref, other_ref, far_ref, out_ref, done_ref):
    done_ref[...] = jnp.zeros(done_ref.shape, F32)
    rows = jnp.concatenate([own_ref[...], other_ref[...], far_ref[...]], 0)
    out_ref[...] = dot_tn(ct_ref[...], rows).astype(BF)


def sum_kernel(got_ref, _done, share_ref, square_ref):
    total = jnp.sum(got_ref[...].astype(F32), axis=0)
    share_ref[...] = total
    square = jnp.sum(jnp.sum(total * total, axis=0, keepdims=True), axis=1, keepdims=True)
    square_ref[...] = jnp.broadcast_to(square, square_ref.shape)


def clip_kernel(squares_ref, share_ref, out_ref):
    total = jnp.sum(squares_ref[...], axis=0, keepdims=True)
    norm = jnp.sqrt(jnp.max(total, axis=1, keepdims=True)) + 1e-06
    value = share_ref[...] / norm
    for m in range(5):
        for r in range(4):
            if m < 4:
                row = (m % 2) * 4 + r
                line = value[row : row + 1, (m // 2) * D : (m // 2 + 1) * D]
            else:
                line = jnp.concatenate(
                    [value[r : r + 1, 2 * D :], value[r + 4 : r + 5, 2 * D :]], 1
                )
            out_ref[m : m + 1, r * D : (r + 1) * D] = line


class Fetched:
    def __init__(self, ref, room, sem):
        self.copy, self.room, self.waited = pltpu.make_async_copy(ref, room, sem), room, False
        self.shape, self.dtype = room.shape, room.dtype
        self.copy.start()

    def __getitem__(self, at):
        if not self.waited:
            self.copy.wait()
            self.waited = True
        return self.room[at]


def call(kernel, outs, *args, smem=(), hbm=(), last=()):
    space = [pltpu.SMEM if i in smem else pltpu.HBM if i in hbm else pltpu.VMEM for i in range(len(args))]
    shapes = [jax.ShapeDtypeStruct(s, d) if i in last else pltpu.VMEM(s, d) for i, (s, d) in enumerate(outs)]
    args = [
        a if i in smem else pltpu.with_memory_space_constraint(a, space[i])
        for i, a in enumerate(args)
    ]

    def whole(*refs):
        refs = list(refs)
        rooms, sems = refs[len(args) + len(outs) : -1], refs[-1]
        for k, i in enumerate(hbm):
            refs[i] = Fetched(refs[i], rooms[k], sems.at[k])
        kernel(*refs[: len(args) + len(outs)])

    out = pl.pallas_call(
        whole if hbm else kernel,
        out_shape=shapes,
        in_specs=[pl.BlockSpec(memory_space=m) for m in space],
        out_specs=[pl.BlockSpec(memory_space=pltpu.VMEM) for _ in outs],
        scratch_shapes=[
            *(pltpu.VMEM(args[i].shape, args[i].dtype) for i in hbm),
            pltpu.SemaphoreType.DMA((len(hbm),)),
        ]
        if hbm
        else (),
        compiler_params=pltpu.CompilerParams(vmem_limit_bytes=24 << 20),
    )(*args)
    return out if len(outs) > 1 else out[0]


def local(
    mesh_latent, grid_cotangent, w_source, w_target, w_node, w_coarse, w_decode,
    neighbour_codes, coarse_ids, edge_source, edge_target, edge_owner,
):
    height, breadth, width = mesh_latent.shape
    nodes = height * breadth
    grid_rows = grid_cotangent.shape[0]
    blocks = edge_owner.shape[0]
    core_pairs = [(0, 1), (1, 0)]
    chip_pairs = [(i, (i + 1) % 32) for i in range(1, 32, 2)]
    chip_pairs += [(b, a) for a, b in chip_pairs]
    done_shape = ((8, 128), F32)

    def other(value):
        return lax.ppermute(value, "c", core_pairs)

    def far(value):
        return lax.ppermute(value, LON, chip_pairs)

    def swapped(value, axes=CHIPS):
        return lax.all_to_all(value, axes, split_axis=0, concat_axis=0, tiled=True)

    h = mesh_latent.reshape(nodes, width)
    ids = jnp.transpose(coarse_ids, (0, 2, 1))
    ids_other = other(ids)
    h_other = other(h)
    above = lax.ppermute(mesh_latent[height - 1], "z", [(i, i + 1) for i in range(3)])
    below = lax.ppermute(mesh_latent[0], "z", [(i + 1, i) for i in range(3)])

    source = edge_source.reshape(blocks, -1)
    target = edge_target.reshape(blocks, -1)
    list_other, list_far, own_target = call(
        lists_kernel,
        [((16, 128), I32), ((16, 128), I32), ((blocks, 128), I32)],
        edge_owner.reshape(blocks), source, target, smem=(0,), hbm=(1, 2),
    )
    list_other = other(list_other)
    list_far = far(list_far)

    pooled = call(
        pool_kernel, [((N_CHIPS * SLOTS, D), BF)], ids, ids_other, h, h_other,
        hbm=(0, 2), last=(0,),
    )
    block = call(halo_kernel, [((BLOCK_ROWS, D), BF)], above, h, below, hbm=(1,))
    block_other = other(block)
    block_far = far(block)
    pooled = swapped(pooled.reshape(N_CHIPS, SLOTS, D))

    block_other_far = other(block_far)
    ct, gs_own, gs_other, gs_far, counted = call(
        counts_kernel,
        [
            ((3 * NODES, grid_rows), BF), ((NODES, D), F32), ((NODES, D), BF), ((NODES, D), BF), done_shape,
        ],
        source, own_target, list_other, list_far, grid_cotangent,
    )
    gs_other = other(gs_other)
    gs_far = far(gs_far)
    coarse = call(coarse_kernel, [((N_CHIPS, SLOTS, D), BF)], pooled, counted, last=(0,))
    coarse = swapped(coarse).reshape(N_CHIPS * SLOTS, D)

    codes_other = other(neighbour_codes)
    around = (block_far, block, block_other, block_other_far)
    slopes, agg = call(
        edges_kernel,
        [((12 * NODES, D), BF), ((2 * NODES, D), BF)],
        neighbour_codes, codes_other, *around, w_source, w_target, hbm=(0, 6, 7),
    )
    gs = gs_own + gs_other.astype(F32) + gs_far.astype(F32)
    gs_pair = other(gs)
    cin = call(
        select_kernel, [((2 * NODES, D), BF)], ids, ids_other, coarse, agg, gs_pair, hbm=(0,),
    )
    cin_other = other(cin)
    mesh_out, message, msg = call(
        main_kernel,
        [((NODES, D), BF), ((NODES, D), BF), ((N_CHIPS * 8, MSG), BF)],
        cin, cin_other, neighbour_codes, codes_other, *around, slopes, agg, gs, gs_pair,
        w_coarse, w_decode, w_node, hbm=(2, 12, 13, 14), last=(0, 1, 2),
    )
    arrived = swapped(msg.reshape(N_CHIPS, 8, MSG))
    grid_out, placed = call(
        grid_kernel, [((grid_rows, D), BF), done_shape],
        ct, message, other(message), far(message), last=(0,),
    )
    share, square = call(sum_kernel, [((8, MSG), F32), ((128, 128), F32)], arrived, placed)
    squares = swapped(square.reshape(128, 1, 128), EVERY).reshape(128, 128)
    clipped = call(clip_kernel, [((5, 4 * D), F32)], squares, share, last=(0,))
    return mesh_out.reshape(height, breadth, width), grid_out, clipped


def solution(mesh):
    split = Mesh(mesh.devices.reshape(4, 4, 4, 2), EVERY)
    return jax.shard_map(
        local,
        mesh=split,
        in_specs=(
            P("z", LON, None),
            P(EVERY, None),
            P(),
            P(),
            P(),
            P(),
            P(),
            P(None, "z", LON),
            P("z", LON, None),
            P(EVERY),
            P(EVERY),
            P(EVERY, None),
        ),
        out_specs=(P("z", LON, None), P(EVERY, None), P(None, EVERY)),
        check_vma=False,
    )
```

```python
import jax
import jax.numpy as jnp
from jax import lax
from jax.experimental import pallas as pl
from jax.experimental.pallas import tpu as pltpu
from jax.sharding import Mesh
from jax.sharding import PartitionSpec as P

CAP = 3
CHIPS = ("z", "y", "x")
LON = ("y", "x", "c")
EVERY = ("z", "y", "x", "c")
BF = jnp.bfloat16
F32 = jnp.float32
I32 = jnp.int32
NODES = 64
D = 512
SLOTS = 8
BLOCK_ROWS = 80
TABLE = 384
N_CHIPS = 64
MSG = 1280


def dot(a, b):
    return jnp.dot(a, b, preferred_element_type=F32)


def dot_nt(a, b):
    return lax.dot_general(a, b, (((1,), (1,)), ((), ())), preferred_element_type=F32)


def dot_tn(a, b):
    return lax.dot_general(a, b, (((0,), (0,)), ((), ())), preferred_element_type=F32)


def iota(shape, dim):
    return lax.broadcasted_iota(I32, shape, dim)


def hot(mask):
    return jnp.where(mask, 1.0, 0.0).astype(BF)


def slope_of(value, sig):
    return sig * (1.0 + value * (1.0 - sig))


def column_of(small):
    rows = small.shape[0]
    count = rows * 8
    spread = dot(hot(iota((count, rows), 0) // 8 == iota((count, rows), 1)), small.astype(F32).astype(BF))
    keep = iota((count, 8), 0) % 8 == iota((count, 8), 1)
    return jnp.sum(jnp.where(keep, spread, 0.0), axis=1, keepdims=True)


def id_columns(ids_ref, core):
    ids = ids_ref[...].reshape(8, 8)
    half = ids >> 1
    chip = column_of(half & 63)
    slot = column_of(half >> 6)
    mine = column_of(ids & 1) == core.astype(F32)
    return chip, slot, mine


def pool_kernel(ids_ref, ids_other_ref, h_ref, h_other_ref, out_ref, chosen_ref):
    core = lax.axis_index("c")
    a = id_columns(ids_ref, core)
    b = id_columns(ids_other_ref, core)
    chip, slot, mine = (jnp.concatenate([u, v], 0) for u, v in zip(a, b))
    base = chip * SLOTS
    place = jnp.where(mine, base + slot, -1.0).astype(I32)
    place_count = jnp.where(mine, base + 6.0, -1.0).astype(I32)
    lanes = iota((2 * NODES, N_CHIPS * SLOTS), 1)
    chosen = hot(lanes == place)
    chosen_ref[...] = chosen
    which = hot(iota((2 * NODES, D), 1) == slot.astype(I32))
    rows = jnp.concatenate([h_ref[...], h_other_ref[...], which], 0)
    out_ref[...] = dot_tn(jnp.concatenate([chosen, hot(lanes == place_count)], 0), rows).astype(BF)


def coarse_kernel(got_ref, out_ref):
    total = jnp.sum(got_ref[...].astype(F32), axis=0)
    counts = jnp.broadcast_to(total[6:7, :], (SLOTS, D))
    keep = iota((SLOTS, D), 0) == iota((SLOTS, D), 1)
    count = jnp.sum(jnp.where(keep, counts, 0.0), axis=1, keepdims=True)
    scale = jnp.where(count > 0.5, lax.rsqrt(jnp.maximum(count, 1.0)), 0.0)
    out_ref[...] = jnp.broadcast_to((total * scale).astype(BF)[None], (N_CHIPS, SLOTS, D))


def select_kernel(chosen_ref, got_ref, _agg, _gs, wc, wd, wn, out_ref, wc_ref, wd_ref, wn_ref, sems):
    copies = [
        pltpu.make_async_copy(a, b, sems.at[i])
        for i, (a, b) in enumerate(((wc, wc_ref), (wd, wd_ref), (wn, wn_ref)))
    ]
    for copy in copies:
        copy.start()
    out_ref[...] = dot(chosen_ref[...], got_ref[...]).astype(BF)
    for copy in copies:
        copy.wait()


def pack_kernel(
    owner_ref, source_ref, target_ref, first_ref, second_ref, h_ref,
    own_ref, other_ref, far_ref, sent_other_ref, sent_far_ref, block_ref,
):
    odd = lax.axis_index("z") % 2 == 1
    first, second = first_ref[...], second_ref[...]
    above = jnp.where(odd, first, second)
    below = jnp.where(odd, second, first)
    block_ref[...] = jnp.concatenate([above, h_ref[...], below], 0)
    lon = lax.axis_index(LON)
    code_other = jnp.where(lax.axis_index("c") == 0, 1, 31)
    lists = (other_ref, far_ref)
    for ref in lists:
        ref[...] = jnp.full(ref.shape, -1, I32)
    ranks = [jnp.int32(0), jnp.int32(0)]
    for b in range(source_ref.shape[0]):
        side = (owner_ref[b] - lon) & 31
        source = source_ref[b : b + 1, :]
        target = target_ref[b : b + 1, :]
        own_ref[b : b + 1, :] = jnp.where(side == 0, target, -1)
        for k, code in enumerate((code_other, 32 - code_other)):
            here = side == code
            place = jnp.where(here, jnp.minimum(ranks[k], 6), 7)
            lists[k][pl.ds(place, 1), :] = source
            lists[k][pl.ds(place + 8, 1), :] = target
            ranks[k] = ranks[k] + here.astype(I32)
    for ref, sent in zip(lists, (sent_other_ref, sent_far_ref)):
        source, target = ref[0:8, :], ref[8:16, :]
        parts = [source, target >> 3, target & 7, jnp.zeros((8, 128), I32)]
        sent[...] = jnp.concatenate([p.astype(F32) for p in parts], 1).astype(BF)


def counted(sources, targets, grid_rows):
    at = iota((grid_rows, 128), 0)
    node = iota((NODES, 128), 0)
    hit = jnp.concatenate([hot(at == t) for t in targets], 1)
    come = jnp.concatenate([hot(node == s) for s in sources], 1)
    return dot_nt(come, hit)


def counts_kernel(
    source_ref, target_ref, other_ref, far_ref, cot_ref, cot_other_ref, cot_far_ref, ct_ref, gs_ref
):
    grid_rows = cot_ref.shape[0]
    step = 4
    total = jnp.zeros((NODES, grid_rows), F32)
    for b in range(0, source_ref.shape[0], step):
        total = total + counted(
            [source_ref[i : i + 1, :] for i in range(b, b + step)],
            [target_ref[i : i + 1, :] for i in range(b, b + step)],
            grid_rows,
        )
    tables = [total.astype(BF)]
    for ref in (other_ref, far_ref):
        tables.append(
            counted(
                [ref[i : i + 1, :] for i in range(CAP)],
                [ref[8 + i : 9 + i, :] for i in range(CAP)],
                grid_rows,
            ).astype(BF)
        )
    ct_ref[...] = tables[0]
    gs_ref[...] = (
        dot(tables[0], cot_ref[...])
        + dot(tables[1], cot_other_ref[...])
        + dot(tables[2], cot_far_ref[...])
    )


def shifted(value, side, core):
    wide = value.astype(F32)
    amount = 4 if side else D - 4
    moved = pltpu.roll(wide, amount, 1)
    lanes = iota(value.shape, 1)
    kept = ((lanes >> 2) & 1) == side
    picked = jnp.where(core == side, wide, moved)
    return jnp.where(kept, picked, 0.0).astype(BF)


def whole_table(refs):
    blocks = [ref[...] for ref in refs]
    return jnp.concatenate([*blocks, jnp.zeros((TABLE - 4 * BLOCK_ROWS, D), BF)], 0)


def chosen_rows(codes_ref, k):
    toward_left = jnp.where(lax.axis_index("c") == 0, -1, 1)
    code = column_of(codes_ref[...].reshape(48, 8)).astype(I32)
    node = iota((6 * NODES, 1), 0) % NODES
    down = (code * 11) >> 5
    row = node // 8 + down
    col = node % 8 + code - 3 * down - 1
    step = jnp.where(col < 0, toward_left, jnp.where(col > 7, -toward_left, 0))
    place = (1 + k + step) * BLOCK_ROWS + row * 8 + (col & 7)
    return hot(iota((6 * NODES, TABLE), 1) == place)


def edges_kernel(
    codes_ref, codes_other_ref, far_ref, own_ref, other_ref, other_far_ref, ws_ref, wt_ref,
    slope_ref, agg_ref,
):
    table = whole_table((far_ref, own_ref, other_ref, other_far_ref))
    for k, (codes, own) in enumerate(((codes_ref, own_ref), (codes_other_ref, other_ref))):
        beside = dot(chosen_rows(codes, k), table).astype(BF)
        toward = dot(own[8:72, :], wt_ref[...])
        pre = dot(beside, ws_ref[...])
        agg = jnp.zeros((NODES, D), F32)
        for s in range(6):
            value = pre[s * NODES : (s + 1) * NODES, :] + toward
            sig = jax.nn.sigmoid(value)
            agg = agg + value * sig
            at = (k * 6 + s) * NODES
            slope_ref[at : at + NODES, :] = slope_of(value, sig).astype(BF)
        agg_ref[k * NODES : (k + 1) * NODES, :] = agg.astype(BF)


def main_kernel(
    cin_ref, cin_other_ref, codes_ref, codes_other_ref, far_ref, own_ref, other_ref, other_far_ref,
    slope_ref, agg_ref, gs_ref, gs_other_ref, wc_ref, wd_ref, wn_ref, sent_far_ref,
    mesh_ref, message_ref, to_far_ref, room,
):
    def leave(lanes, value):
        room[:, lanes] = value.astype(BF)

    core = lax.axis_index("c")
    chosen = jnp.concatenate([chosen_rows(codes_ref, 0), chosen_rows(codes_other_ref, 1)], 0)
    cin = jnp.concatenate(
        [
            cin_ref[:NODES, :].astype(F32) + cin_other_ref[NODES:, :].astype(F32),
            cin_ref[NODES:, :].astype(F32) + cin_other_ref[:NODES, :].astype(F32),
        ],
        0,
    ).astype(BF)
    h = jnp.concatenate([own_ref[8:72, :], other_ref[8:72, :]], 0)
    cpre = dot(cin, wc_ref[...])
    csig = jax.nn.sigmoid(cpre)
    npre = dot(agg_ref[...], wn_ref[...]) + (cpre * csig).astype(BF).astype(F32)
    nsig = jax.nn.sigmoid(npre)
    mesh_out = (h.astype(F32) + npre * nsig).astype(BF)
    mesh_ref[...] = mesh_out[:NODES, :]
    pre = dot(mesh_out, wd_ref[...])
    sig = jax.nn.sigmoid(pre)
    message = (pre * sig).astype(BF)
    message_ref[...] = message
    to_far_ref[...] = jnp.concatenate([message[:NODES, :], sent_far_ref[...]], 0)
    gs = jnp.concatenate([gs_ref[...], gs_other_ref[...]], 0)
    d_source = (gs * slope_of(pre, sig)).astype(BF)
    d_out = dot_nt(d_source, wd_ref[...])
    d_node = (d_out * slope_of(npre, nsig)).astype(BF)
    leave(
        pl.ds(2 * D, D // 2),
        dot_tn(
            jnp.concatenate([shifted(mesh_out, 0, core), shifted(mesh_out, 1, core)], 0),
            jnp.concatenate([d_source[:, : D // 2], d_source[:, D // 2 :]], 0),
        ),
    )
    d_agg = dot_nt(d_node, wn_ref[...])
    d_coarse = (d_node.astype(F32) * slope_of(cpre, csig)).astype(BF)
    leave(
        pl.ds(D, D),
        dot_tn(
            jnp.concatenate([shifted(agg_ref[...], 0, core), shifted(cin, 1, core)], 0),
            jnp.concatenate([d_node, d_coarse], 0),
        ),
    )
    d_edges, sums = [], []
    for k in range(2):
        part = d_agg[k * NODES : (k + 1) * NODES, :]
        d_sum = jnp.zeros((NODES, D), F32)
        for s in range(6):
            at = (k * 6 + s) * NODES
            d_edge = (part * slope_ref[at : at + NODES, :].astype(F32)).astype(BF)
            d_sum = d_sum + d_edge.astype(F32)
            d_edges.append(d_edge)
        sums.append(d_sum.astype(BF))
    scattered = dot_tn(chosen, jnp.concatenate(d_edges, 0)).astype(BF)
    table = whole_table((far_ref, own_ref, other_ref, other_far_ref))
    leave(
        pl.ds(0, D),
        dot_tn(
            jnp.concatenate([shifted(table, 0, core), shifted(h, 1, core)], 0),
            jnp.concatenate([scattered, *sums], 0),
        ),
    )


def grid_kernel(ct_ref, message_ref, lists_ref, far_ref, out_ref, done_ref):
    done_ref[...] = jnp.zeros(done_ref.shape, F32)
    grid_rows = out_ref.shape[0]
    tables = [ct_ref[...]]
    for lists in (lists_ref[...], far_ref[NODES : NODES + 8, :]):
        lists = lists.astype(F32)
        source = lists[:, 0:128].astype(I32)
        target = (lists[:, 128:256] * 8.0 + lists[:, 256:384]).astype(I32)
        tables.append(
            counted(
                [source[i : i + 1, :] for i in range(CAP)],
                [target[i : i + 1, :] for i in range(CAP)],
                grid_rows,
            ).astype(BF)
        )
    rows = jnp.concatenate([message_ref[...], far_ref[0:NODES, :]], 0)
    out_ref[...] = dot_tn(jnp.concatenate(tables, 0), rows).astype(BF)


def sum_kernel(got_ref, share_ref, square_ref):
    total = jnp.sum(got_ref[...].astype(F32), axis=0)
    share_ref[...] = total
    square = jnp.sum(jnp.sum(total * total, axis=0, keepdims=True), axis=1, keepdims=True)
    square_ref[...] = jnp.broadcast_to(square, square_ref.shape)


def clip_kernel(squares_ref, share_ref, _done, out_ref):
    total = jnp.sum(squares_ref[...], axis=0, keepdims=True)
    norm = jnp.sqrt(jnp.max(total, axis=1, keepdims=True)) + 1e-06
    value = share_ref[...] / norm
    for m in range(5):
        for r in range(4):
            if m < 4:
                row = (m % 2) * 4 + r
                line = value[row : row + 1, (m // 2) * D : (m // 2 + 1) * D]
            else:
                line = jnp.concatenate(
                    [value[r : r + 1, 2 * D :], value[r + 4 : r + 5, 2 * D :]], 1
                )
            out_ref[m : m + 1, r * D : (r + 1) * D] = line


class Fetched:
    def __init__(self, ref, room, sem):
        self.copy, self.room, self.waited = pltpu.make_async_copy(ref, room, sem), room, False
        self.shape, self.dtype = room.shape, room.dtype
        self.copy.start()

    def __getitem__(self, at):
        if not self.waited:
            self.copy.wait()
            self.waited = True
        return self.room[at]


def call(kernel, outs, *args, smem=(), hbm=(), raw=(), last=(), raw_out=(), scratch=()):
    space = [
        pltpu.SMEM if i in smem else pltpu.HBM if i in hbm or i in raw else pltpu.VMEM
        for i in range(len(args))
    ]
    shapes = [
        pltpu.HBM(s, d) if i in raw_out else jax.ShapeDtypeStruct(s, d) if i in last else pltpu.VMEM(s, d)
        for i, (s, d) in enumerate(outs)
    ]
    args = [
        a if i in smem else pltpu.with_memory_space_constraint(a, space[i])
        for i, a in enumerate(args)
    ]
    ends = len(args) + len(outs)

    def whole(*refs):
        refs = list(refs)
        own, rooms, sems = refs[ends : ends + len(scratch)], refs[ends + len(scratch) : -1], refs[-1]
        for k, i in enumerate(hbm):
            refs[i] = Fetched(refs[i], rooms[k], sems.at[k])
        kernel(*refs[:ends], *own)

    out = pl.pallas_call(
        whole if hbm else kernel,
        out_shape=shapes,
        in_specs=[pl.BlockSpec(memory_space=m) for m in space],
        out_specs=[
            pl.BlockSpec(memory_space=pltpu.HBM if i in raw_out else pltpu.VMEM) for i in range(len(outs))
        ],
        scratch_shapes=[
            *scratch,
            *(
                [
                    *(pltpu.VMEM(args[i].shape, args[i].dtype) for i in hbm),
                    pltpu.SemaphoreType.DMA((len(hbm),)),
                ]
                if hbm
                else ()
            ),
        ],
        compiler_params=pltpu.CompilerParams(vmem_limit_bytes=24 << 20),
    )(*args)
    return out if len(outs) > 1 else out[0]


def local(
    mesh_latent, grid_cotangent, w_source, w_target, w_node, w_coarse, w_decode,
    neighbour_codes, coarse_ids, edge_source, edge_target, edge_owner,
):
    height, breadth, width = mesh_latent.shape
    nodes = height * breadth
    grid_rows = grid_cotangent.shape[0]
    blocks = edge_owner.shape[0]
    core_pairs = [(0, 1), (1, 0)]
    chip_pairs = [(i, (i + 1) % 32) for i in range(1, 32, 2)]
    chip_pairs += [(b, a) for a, b in chip_pairs]
    done_shape = ((8, 128), F32)

    def other(value):
        return lax.ppermute(value, "c", core_pairs)

    def far(value):
        return lax.ppermute(value, LON, chip_pairs)

    def swapped(value, axes=CHIPS):
        return lax.all_to_all(value, axes, split_axis=0, concat_axis=0, tiled=True)

    h = mesh_latent.reshape(nodes, width)
    ids = jnp.transpose(coarse_ids, (0, 2, 1))
    ids_other = other(ids)
    h_other = other(h)
    odd = lax.axis_index("z") % 2 == 1
    top, bottom = mesh_latent[0], mesh_latent[height - 1]
    first = lax.ppermute(jnp.where(odd, top, bottom), "z", [(0, 1), (1, 0), (2, 3), (3, 2)])
    second = lax.ppermute(jnp.where(odd, bottom, top), "z", [(1, 2), (2, 1)])
    pooled, chosen = call(
        pool_kernel, [((N_CHIPS * SLOTS, D), BF), ((2 * NODES, N_CHIPS * SLOTS), BF)],
        ids, ids_other, h, h_other, hbm=(0, 2), last=(0,),
    )
    pooled = swapped(pooled.reshape(N_CHIPS, SLOTS, D))

    source = edge_source.reshape(blocks, -1)
    target = edge_target.reshape(blocks, -1)
    lists = ((16, 128), I32)
    own_target, list_other, list_far, sent_other, sent_far, block = call(
        pack_kernel,
        [
            ((blocks, 128), I32), lists, lists, ((8, D), BF), ((8, D), BF), ((BLOCK_ROWS, D), BF),
        ],
        edge_owner.reshape(blocks), source, target, first, second, h, smem=(0,), hbm=(1, 2, 5),
    )
    cot_far = far(grid_cotangent)
    block_far = far(block)
    cot_other = other(grid_cotangent)
    block_other = other(block)
    codes_other = other(neighbour_codes)
    lists_other = other(sent_other)
    coarse = call(coarse_kernel, [((N_CHIPS, SLOTS, D), BF)], pooled, last=(0,))
    coarse = swapped(coarse).reshape(N_CHIPS * SLOTS, D)

    ct, gs = call(
        counts_kernel,
        [((NODES, grid_rows), BF), ((NODES, D), F32)],
        source, own_target, list_other, list_far, grid_cotangent, cot_other, cot_far, hbm=(0, 4, 5, 6),
    )
    block_other_far = other(block_far)
    gs_pair = other(gs)
    around = (block_far, block, block_other, block_other_far)
    slopes, agg = call(
        edges_kernel,
        [((12 * NODES, D), BF), ((2 * NODES, D), BF)],
        neighbour_codes, codes_other, *around, w_source, w_target, hbm=(0, 6, 7),
    )
    weight = (w_coarse.shape, BF)
    cin, wc, wd, wn = call(
        select_kernel, [((2 * NODES, D), BF), weight, weight, weight],
        chosen, coarse, agg, gs_pair, w_coarse, w_decode, w_node,
        raw=(4, 5, 6), scratch=(pltpu.SemaphoreType.DMA((3,)),),
    )
    cin_other = other(cin)
    sent = ((NODES + 8, D), BF)
    mesh_out, message, to_far, msg = call(
        main_kernel,
        [((NODES, D), BF), ((2 * NODES, D), BF), sent, ((N_CHIPS * 8, MSG), BF)],
        cin, cin_other, neighbour_codes, codes_other, *around, slopes, agg, gs, gs_pair,
        wc, wd, wn, sent_far,
        hbm=(2,), last=(0, 3),
    )
    arrived = swapped(msg.reshape(N_CHIPS, 8, MSG))
    got_far = far(to_far)
    share, square = call(sum_kernel, [((8, MSG), F32), ((128, 128), F32)], arrived)
    squares = swapped(square.reshape(128, 1, 128), EVERY).reshape(128, 128)
    grid_out, placed = call(
        grid_kernel, [((grid_rows, D), BF), done_shape], ct, message, lists_other, got_far, last=(0,),
    )
    clipped = call(clip_kernel, [((5, 4 * D), F32)], squares, share, placed, last=(0,))
    return mesh_out.reshape(height, breadth, width), grid_out, clipped


def solution(mesh):
    split = Mesh(mesh.devices.reshape(4, 4, 4, 2), EVERY)
    return jax.shard_map(
        local,
        mesh=split,
        in_specs=(
            P("z", LON, None),
            P(EVERY, None),
            P(),
            P(),
            P(),
            P(),
            P(),
            P(None, "z", LON),
            P("z", LON, None),
            P(EVERY),
            P(EVERY),
            P(EVERY, None),
        ),
        out_specs=(P("z", LON, None), P(EVERY, None), P(None, EVERY)),
        check_vma=False,
    )
```

```python
import jax
import jax.numpy as jnp
from jax import lax
from jax.experimental import pallas as pl
from jax.experimental.pallas import tpu as pltpu
from jax.sharding import Mesh
from jax.sharding import PartitionSpec as P

CAP = 3
CHIPS = ("z", "y", "x")
LON = ("y", "x", "c")
EVERY = ("z", "y", "x", "c")
BF = jnp.bfloat16
F32 = jnp.float32
I32 = jnp.int32
NODES = 64
D = 512
SLOTS = 8
CHUNK = 384
BLOCK_ROWS = 80
TABLE = 384
N_CHIPS = 64
MSG = 1280


def dot(a, b):
    return jnp.dot(a, b, preferred_element_type=F32)


def dot_nt(a, b):
    return lax.dot_general(a, b, (((1,), (1,)), ((), ())), preferred_element_type=F32)


def dot_tn(a, b):
    return lax.dot_general(a, b, (((0,), (0,)), ((), ())), preferred_element_type=F32)


def iota(shape, dim):
    return lax.broadcasted_iota(I32, shape, dim)


def hot(mask):
    return jnp.where(mask, 1.0, 0.0).astype(BF)


def slope_of(value, sig):
    return sig * (1.0 + value * (1.0 - sig))


def column_of(small):
    rows = small.shape[0]
    count = rows * 8
    spread = dot(hot(iota((count, rows), 0) // 8 == iota((count, rows), 1)), small.astype(F32).astype(BF))
    keep = iota((count, 8), 0) % 8 == iota((count, 8), 1)
    return jnp.sum(jnp.where(keep, spread, 0.0), axis=1, keepdims=True)


def id_columns(ids_ref, core):
    ids = ids_ref[...].reshape(8, 8)
    half = ids >> 1
    chip = column_of(half & 63)
    slot = column_of(half >> 6)
    mine = jnp.where(column_of(ids & 1) == core.astype(F32), 1.0, 0.0)
    return chip, slot, mine


def routes(chip, slot, mine):
    lanes = iota((2 * NODES, N_CHIPS * SLOTS), 1)
    chip, slot = chip.astype(I32), slot.astype(I32)
    usual = mine & (slot < 5)
    extra = mine & (slot >= 5)
    main = hot(lanes == jnp.where(usual, chip * SLOTS + slot, -1))
    tails = [
        hot(lanes == jnp.where(usual & (slot >> 1 == t), chip * SLOTS + 6 + (slot & 1), -1)) for t in range(3)
    ]
    count = jnp.where(usual, chip * SLOTS + 5, -1)
    quarters = [hot(lanes == jnp.where(extra, k * SLOTS + 5, -1)) for k in range(4)]
    counts = hot((lanes == count) | (extra & ((lanes & 7) == 5) & (lanes < 4 * SLOTS)))
    return main, tails, quarters, counts


def pool_kernel(ids_ref, ids_other_ref, h_ref, h_other_ref, out_ref, info_ref):
    core = lax.axis_index("c")
    a = id_columns(ids_ref, core)
    b = id_columns(ids_other_ref, core)
    chip, slot, mine = (jnp.concatenate([u, v], 0) for u, v in zip(a, b))
    at = iota(info_ref.shape, 1)
    mine = mine > 0.5
    info_ref[...] = jnp.where(at == 0, chip, jnp.where(at == 1, slot, jnp.where(mine, 1.0, 0.0)))
    main, tails, quarters, counts = routes(chip, slot, mine)
    which = hot(iota((2 * NODES, 128), 1) == slot.astype(I32))
    h = jnp.concatenate([h_ref[...], h_other_ref[...]], 0)
    tile = [h[:, 128 * k : 128 * (k + 1)] for k in range(4)]
    terms = [[(main, tile[t]), (tails[t], tile[3])] for t in range(3)]
    terms[0].append((counts, which))
    terms[1] += list(zip(quarters, tile))
    for t in range(3):
        left, right = zip(*terms[t])
        out_ref[:, 128 * t : 128 * (t + 1)] = dot_tn(
            jnp.concatenate(left, 0), jnp.concatenate(right, 0)
        ).astype(BF)


def coarse_kernel(got_ref, out_ref):
    total = jnp.sum(got_ref[...].astype(F32), axis=0)
    row = iota((SLOTS, 128), 0)
    tail = jnp.zeros((SLOTS, 128), F32)
    for s in range(5):
        line = total[6 + s % 2 : 7 + s % 2, 128 * (s // 2) : 128 * (s // 2 + 1)]
        tail = jnp.where(row == s, jnp.broadcast_to(line, tail.shape), tail)
    counts = jnp.broadcast_to(total[5:6, 0:128], (SLOTS, 128))
    count = jnp.sum(jnp.where(row == iota((SLOTS, 128), 1), counts, 0.0), axis=1, keepdims=True)
    scale = jnp.where(count > 0.5, lax.rsqrt(jnp.maximum(count, 1.0)), 0.0)
    body, tail = total * scale, tail * scale
    parts = []
    for t in range(3):
        even = jnp.broadcast_to(tail[2 * t : 2 * t + 1, :], tail.shape)
        uneven = jnp.broadcast_to(tail[2 * t + 1 : 2 * t + 2, :], tail.shape)
        part = body[:, 128 * t : 128 * (t + 1)]
        parts.append(jnp.where(row < 6, part, jnp.where(row == 6, even, uneven)))
    packed = jnp.concatenate(parts, 1).astype(BF)
    out_ref[...] = jnp.broadcast_to(packed[None], out_ref.shape)


def select_kernel(info_ref, got_ref, _agg, _gs, wc, wd, wn, out_ref, wc_ref, wd_ref, wn_ref, sems):
    copies = [
        pltpu.make_async_copy(a, b, sems.at[i])
        for i, (a, b) in enumerate(((wc, wc_ref), (wd, wd_ref), (wn, wn_ref)))
    ]
    for copy in copies:
        copy.start()
    info = info_ref[...]
    main, tails, quarters, _ = routes(info[:, 0:1], info[:, 1:2], info[:, 2:3] > 0.5)
    got = got_ref[...]
    tile = [got[:, 128 * t : 128 * (t + 1)] for t in range(3)]
    parts = [
        dot(jnp.concatenate([main, quarters[t]], 1), jnp.concatenate([tile[t], tile[1]], 0)) for t in range(3)
    ]
    parts.append(dot(jnp.concatenate([*tails, quarters[3]], 1), jnp.concatenate([*tile, tile[1]], 0)))
    out_ref[...] = jnp.concatenate(parts, 1).astype(BF)
    for copy in copies:
        copy.wait()


def pack_kernel(
    owner_ref, source_ref, target_ref, first_ref, second_ref, h_ref,
    own_ref, other_ref, far_ref, sent_other_ref, sent_far_ref, block_ref,
):
    odd = lax.axis_index("z") % 2 == 1
    first, second = first_ref[...], second_ref[...]
    above = jnp.where(odd, first, second)
    below = jnp.where(odd, second, first)
    block_ref[...] = jnp.concatenate([above, h_ref[...], below], 0)
    lon = lax.axis_index(LON)
    code_other = jnp.where(lax.axis_index("c") == 0, 1, 31)
    lists = (other_ref, far_ref)
    for ref in lists:
        ref[...] = jnp.full(ref.shape, -1, I32)
    ranks = [jnp.int32(0), jnp.int32(0)]
    for b in range(source_ref.shape[0]):
        side = (owner_ref[b] - lon) & 31
        source = source_ref[b : b + 1, :]
        target = target_ref[b : b + 1, :]
        own_ref[b : b + 1, :] = jnp.where(side == 0, target, -1)
        for k, code in enumerate((code_other, 32 - code_other)):
            here = side == code
            place = jnp.where(here, jnp.minimum(ranks[k], 6), 7)
            lists[k][pl.ds(place, 1), :] = source
            lists[k][pl.ds(place + 8, 1), :] = target
            ranks[k] = ranks[k] + here.astype(I32)
    for ref, sent in zip(lists, (sent_other_ref, sent_far_ref)):
        source, target = ref[0:8, :], ref[8:16, :]
        parts = [source, target >> 3, target & 7, jnp.zeros((8, 128), I32)]
        sent[...] = jnp.concatenate([p.astype(F32) for p in parts], 1).astype(BF)


def counted(sources, targets, grid_rows):
    at = iota((grid_rows, 128), 0)
    node = iota((NODES, 128), 0)
    hit = jnp.concatenate([hot(at == t) for t in targets], 1)
    come = jnp.concatenate([hot(node == s) for s in sources], 1)
    return dot_nt(come, hit)


def tally_kernel(source_ref, target_ref, other_ref, far_ref, ct_ref):
    grid_rows = ct_ref.shape[1]
    step = 4
    total = jnp.zeros((NODES, grid_rows), F32)
    for b in range(0, source_ref.shape[0], step):
        total = total + counted(
            [source_ref[i : i + 1, :] for i in range(b, b + step)],
            [target_ref[i : i + 1, :] for i in range(b, b + step)],
            grid_rows,
        )
    ct_ref[0:NODES, :] = total.astype(BF)
    for k, ref in enumerate((other_ref, far_ref)):
        ct_ref[(k + 1) * NODES : (k + 2) * NODES, :] = counted(
            [ref[i : i + 1, :] for i in range(CAP)],
            [ref[8 + i : 9 + i, :] for i in range(CAP)],
            grid_rows,
        ).astype(BF)


def gather_kernel(ct_ref, cot_ref, cot_other_ref, cot_far_ref, gs_ref):
    total = dot(ct_ref[NODES : 2 * NODES, :], cot_other_ref[...])
    total = total + dot(ct_ref[2 * NODES : 3 * NODES, :], cot_far_ref[...])
    gs_ref[...] = total + dot(ct_ref[0:NODES, :], cot_ref[...])


def shifted(value, side, core):
    wide = value.astype(F32)
    amount = 4 if side else D - 4
    moved = pltpu.roll(wide, amount, 1)
    lanes = iota(value.shape, 1)
    kept = ((lanes >> 2) & 1) == side
    picked = jnp.where(core == side, wide, moved)
    return jnp.where(kept, picked, 0.0).astype(BF)


def whole_table(refs):
    blocks = [ref[...] for ref in refs]
    return jnp.concatenate([*blocks, jnp.zeros((TABLE - 4 * BLOCK_ROWS, D), BF)], 0)


def chosen_rows(codes_ref, k):
    toward_left = jnp.where(lax.axis_index("c") == 0, -1, 1)
    code = column_of(codes_ref[...].reshape(48, 8)).astype(I32)
    node = iota((6 * NODES, 1), 0) % NODES
    down = (code * 11) >> 5
    row = node // 8 + down
    col = node % 8 + code - 3 * down - 1
    step = jnp.where(col < 0, toward_left, jnp.where(col > 7, -toward_left, 0))
    place = (1 + k + step) * BLOCK_ROWS + row * 8 + (col & 7)
    return hot(iota((6 * NODES, TABLE), 1) == place)


def edges_kernel(
    codes_ref, codes_other_ref, far_ref, own_ref, other_ref, other_far_ref, ws_ref, wt_ref,
    slope_ref, agg_ref,
):
    table = whole_table((far_ref, own_ref, other_ref, other_far_ref))
    for k, (codes, own) in enumerate(((codes_ref, own_ref), (codes_other_ref, other_ref))):
        beside = dot(chosen_rows(codes, k), table).astype(BF)
        toward = dot(own[8:72, :], wt_ref[...])
        pre = dot(beside, ws_ref[...])
        agg = jnp.zeros((NODES, D), F32)
        for s in range(6):
            value = pre[s * NODES : (s + 1) * NODES, :] + toward
            sig = jax.nn.sigmoid(value)
            agg = agg + value * sig
            at = (k * 6 + s) * NODES
            slope_ref[at : at + NODES, :] = slope_of(value, sig).astype(BF)
        agg_ref[k * NODES : (k + 1) * NODES, :] = agg.astype(BF)


def main_kernel(
    cin_ref, cin_other_ref, codes_ref, codes_other_ref, far_ref, own_ref, other_ref, other_far_ref,
    slope_ref, agg_ref, gs_ref, gs_other_ref, wc_ref, wd_ref, wn_ref, sent_far_ref,
    mesh_ref, message_ref, to_far_ref, room,
):
    def leave(lanes, value):
        room[:, lanes] = value.astype(BF)

    core = lax.axis_index("c")
    chosen = jnp.concatenate([chosen_rows(codes_ref, 0), chosen_rows(codes_other_ref, 1)], 0)
    cin = jnp.concatenate(
        [
            cin_ref[:NODES, :].astype(F32) + cin_other_ref[NODES:, :].astype(F32),
            cin_ref[NODES:, :].astype(F32) + cin_other_ref[:NODES, :].astype(F32),
        ],
        0,
    ).astype(BF)
    h = jnp.concatenate([own_ref[8:72, :], other_ref[8:72, :]], 0)
    cpre = dot(cin, wc_ref[...])
    csig = jax.nn.sigmoid(cpre)
    npre = dot(agg_ref[...], wn_ref[...]) + (cpre * csig).astype(BF).astype(F32)
    nsig = jax.nn.sigmoid(npre)
    mesh_out = (h.astype(F32) + npre * nsig).astype(BF)
    mesh_ref[...] = mesh_out[:NODES, :]
    pre = dot(mesh_out, wd_ref[...])
    sig = jax.nn.sigmoid(pre)
    message = (pre * sig).astype(BF)
    message_ref[...] = message
    to_far_ref[...] = jnp.concatenate([message[:NODES, :], sent_far_ref[...]], 0)
    gs = jnp.concatenate([gs_ref[...], gs_other_ref[...]], 0)
    d_source = (gs * slope_of(pre, sig)).astype(BF)
    d_out = dot_nt(d_source, wd_ref[...])
    d_node = (d_out * slope_of(npre, nsig)).astype(BF)
    leave(
        pl.ds(2 * D, D // 2),
        dot_tn(
            jnp.concatenate([shifted(mesh_out, 0, core), shifted(mesh_out, 1, core)], 0),
            jnp.concatenate([d_source[:, : D // 2], d_source[:, D // 2 :]], 0),
        ),
    )
    d_agg = dot_nt(d_node, wn_ref[...])
    d_coarse = (d_node.astype(F32) * slope_of(cpre, csig)).astype(BF)
    leave(
        pl.ds(D, D),
        dot_tn(
            jnp.concatenate([shifted(agg_ref[...], 0, core), shifted(cin, 1, core)], 0),
            jnp.concatenate([d_node, d_coarse], 0),
        ),
    )
    d_edges, sums = [], []
    for k in range(2):
        part = d_agg[k * NODES : (k + 1) * NODES, :]
        d_sum = jnp.zeros((NODES, D), F32)
        for s in range(6):
            at = (k * 6 + s) * NODES
            d_edge = (part * slope_ref[at : at + NODES, :].astype(F32)).astype(BF)
            d_sum = d_sum + d_edge.astype(F32)
            d_edges.append(d_edge)
        sums.append(d_sum.astype(BF))
    scattered = dot_tn(chosen, jnp.concatenate(d_edges, 0)).astype(BF)
    table = whole_table((far_ref, own_ref, other_ref, other_far_ref))
    leave(
        pl.ds(0, D),
        dot_tn(
            jnp.concatenate([shifted(table, 0, core), shifted(h, 1, core)], 0),
            jnp.concatenate([scattered, *sums], 0),
        ),
    )


def grid_kernel(ct_ref, message_ref, lists_ref, far_ref, out_ref, done_ref):
    done_ref[...] = jnp.zeros(done_ref.shape, F32)
    grid_rows = out_ref.shape[0]
    tables = [ct_ref[0:NODES, :]]
    for lists in (lists_ref[...], far_ref[NODES : NODES + 8, :]):
        lists = lists.astype(F32)
        source = lists[:, 0:128].astype(I32)
        target = (lists[:, 128:256] * 8.0 + lists[:, 256:384]).astype(I32)
        tables.append(
            counted(
                [source[i : i + 1, :] for i in range(CAP)],
                [target[i : i + 1, :] for i in range(CAP)],
                grid_rows,
            ).astype(BF)
        )
    rows = jnp.concatenate([message_ref[...], far_ref[0:NODES, :]], 0)
    out_ref[...] = dot_tn(jnp.concatenate(tables, 0), rows).astype(BF)


def sum_kernel(got_ref, share_ref, square_ref):
    total = jnp.sum(got_ref[...].astype(F32), axis=0)
    share_ref[...] = total
    square = jnp.sum(jnp.sum(total * total, axis=0, keepdims=True), axis=1, keepdims=True)
    square_ref[...] = jnp.broadcast_to(square, square_ref.shape)


def clip_kernel(squares_ref, share_ref, _done, out_ref):
    total = jnp.sum(squares_ref[...], axis=0, keepdims=True)
    norm = jnp.sqrt(jnp.max(total, axis=1, keepdims=True)) + 1e-06
    value = share_ref[...] / norm
    for m in range(5):
        for r in range(4):
            if m < 4:
                row = (m % 2) * 4 + r
                line = value[row : row + 1, (m // 2) * D : (m // 2 + 1) * D]
            else:
                line = jnp.concatenate(
                    [value[r : r + 1, 2 * D :], value[r + 4 : r + 5, 2 * D :]], 1
                )
            out_ref[m : m + 1, r * D : (r + 1) * D] = line


class Fetched:
    def __init__(self, ref, room, sem):
        self.copy, self.room, self.waited = pltpu.make_async_copy(ref, room, sem), room, False
        self.shape, self.dtype = room.shape, room.dtype
        self.copy.start()

    def __getitem__(self, at):
        if not self.waited:
            self.copy.wait()
            self.waited = True
        return self.room[at]


def call(kernel, outs, *args, smem=(), hbm=(), raw=(), last=(), raw_out=(), scratch=()):
    space = [
        pltpu.SMEM if i in smem else pltpu.HBM if i in hbm or i in raw else pltpu.VMEM
        for i in range(len(args))
    ]
    shapes = [
        pltpu.HBM(s, d) if i in raw_out else jax.ShapeDtypeStruct(s, d) if i in last else pltpu.VMEM(s, d)
        for i, (s, d) in enumerate(outs)
    ]
    args = [
        a if i in smem else pltpu.with_memory_space_constraint(a, space[i])
        for i, a in enumerate(args)
    ]
    ends = len(args) + len(outs)

    def whole(*refs):
        refs = list(refs)
        own, rooms, sems = refs[ends : ends + len(scratch)], refs[ends + len(scratch) : -1], refs[-1]
        for k, i in enumerate(hbm):
            refs[i] = Fetched(refs[i], rooms[k], sems.at[k])
        kernel(*refs[:ends], *own)

    out = pl.pallas_call(
        whole if hbm else kernel,
        out_shape=shapes,
        in_specs=[pl.BlockSpec(memory_space=m) for m in space],
        out_specs=[
            pl.BlockSpec(memory_space=pltpu.HBM if i in raw_out else pltpu.VMEM) for i in range(len(outs))
        ],
        scratch_shapes=[
            *scratch,
            *(
                [
                    *(pltpu.VMEM(args[i].shape, args[i].dtype) for i in hbm),
                    pltpu.SemaphoreType.DMA((len(hbm),)),
                ]
                if hbm
                else ()
            ),
        ],
        compiler_params=pltpu.CompilerParams(vmem_limit_bytes=24 << 20),
    )(*args)
    return out if len(outs) > 1 else out[0]


def local(
    mesh_latent, grid_cotangent, w_source, w_target, w_node, w_coarse, w_decode,
    neighbour_codes, coarse_ids, edge_source, edge_target, edge_owner,
):
    height, breadth, width = mesh_latent.shape
    nodes = height * breadth
    grid_rows = grid_cotangent.shape[0]
    blocks = edge_owner.shape[0]
    core_pairs = [(0, 1), (1, 0)]
    chip_pairs = [(i, (i + 1) % 32) for i in range(1, 32, 2)]
    chip_pairs += [(b, a) for a, b in chip_pairs]
    done_shape = ((8, 128), F32)

    def other(value):
        return lax.ppermute(value, "c", core_pairs)

    def far(value):
        return lax.ppermute(value, LON, chip_pairs)

    def swapped(value, axes=CHIPS):
        return lax.all_to_all(value, axes, split_axis=0, concat_axis=0, tiled=True)

    h = mesh_latent.reshape(nodes, width)
    ids = jnp.transpose(coarse_ids, (0, 2, 1))
    ids_other = other(ids)
    h_other = other(h)
    odd = lax.axis_index("z") % 2 == 1
    top, bottom = mesh_latent[0], mesh_latent[height - 1]
    first = lax.ppermute(jnp.where(odd, top, bottom), "z", [(0, 1), (1, 0), (2, 3), (3, 2)])
    second = lax.ppermute(jnp.where(odd, bottom, top), "z", [(1, 2), (2, 1)])
    pooled, info = call(
        pool_kernel, [((N_CHIPS * SLOTS, CHUNK), BF), ((2 * NODES, 128), F32)],
        ids, ids_other, h, h_other, hbm=(0, 2), last=(0,),
    )
    pooled = swapped(pooled.reshape(N_CHIPS, SLOTS, CHUNK))

    source = edge_source.reshape(blocks, -1)
    target = edge_target.reshape(blocks, -1)
    lists = ((16, 128), I32)
    own_target, list_other, list_far, sent_other, sent_far, block = call(
        pack_kernel,
        [
            ((blocks, 128), I32), lists, lists, ((8, D), BF), ((8, D), BF), ((BLOCK_ROWS, D), BF),
        ],
        edge_owner.reshape(blocks), source, target, first, second, h, smem=(0,), hbm=(1, 2, 5),
    )
    cot_far = far(grid_cotangent)
    block_far = far(block)
    cot_other = other(grid_cotangent)
    block_other = other(block)
    codes_other = other(neighbour_codes)
    lists_other = other(sent_other)
    ct = call(
        tally_kernel, [((3 * NODES, grid_rows), BF)],
        source, own_target, list_other, list_far, hbm=(0,),
    )
    coarse = call(coarse_kernel, [((N_CHIPS, SLOTS, CHUNK), BF)], pooled, last=(0,))
    coarse = swapped(coarse).reshape(N_CHIPS * SLOTS, CHUNK)

    gs = call(
        gather_kernel, [((NODES, D), F32)], ct, grid_cotangent, cot_other, cot_far, hbm=(1,)
    )
    block_other_far = other(block_far)
    gs_pair = other(gs)
    around = (block_far, block, block_other, block_other_far)
    slopes, agg = call(
        edges_kernel,
        [((12 * NODES, D), BF), ((2 * NODES, D), BF)],
        neighbour_codes, codes_other, *around, w_source, w_target, hbm=(0, 6, 7),
    )
    weight = (w_coarse.shape, BF)
    cin, wc, wd, wn = call(
        select_kernel, [((2 * NODES, D), BF), weight, weight, weight],
        info, coarse, agg, gs_pair, w_coarse, w_decode, w_node,
        raw=(4, 5, 6), scratch=(pltpu.SemaphoreType.DMA((3,)),),
    )
    cin_other = other(cin)
    sent = ((NODES + 8, D), BF)
    mesh_out, message, to_far, msg = call(
        main_kernel,
        [((NODES, D), BF), ((2 * NODES, D), BF), sent, ((N_CHIPS * 8, MSG), BF)],
        cin, cin_other, neighbour_codes, codes_other, *around, slopes, agg, gs, gs_pair,
        wc, wd, wn, sent_far,
        hbm=(2,), last=(0, 3),
    )
    arrived = swapped(msg.reshape(N_CHIPS, 8, MSG))
    got_far = far(to_far)
    share, square = call(sum_kernel, [((8, MSG), F32), ((128, 128), F32)], arrived)
    squares = swapped(square.reshape(128, 1, 128), EVERY).reshape(128, 128)
    grid_out, placed = call(
        grid_kernel, [((grid_rows, D), BF), done_shape], ct, message, lists_other, got_far, last=(0,),
    )
    clipped = call(clip_kernel, [((5, 4 * D), F32)], squares, share, placed, last=(0,))
    return mesh_out.reshape(height, breadth, width), grid_out, clipped


def solution(mesh):
    split = Mesh(mesh.devices.reshape(4, 4, 4, 2), EVERY)
    return jax.shard_map(
        local,
        mesh=split,
        in_specs=(
            P("z", LON, None),
            P(EVERY, None),
            P(),
            P(),
            P(),
            P(),
            P(),
            P(None, "z", LON),
            P("z", LON, None),
            P(EVERY),
            P(EVERY),
            P(EVERY, None),
        ),
        out_specs=(P("z", LON, None), P(EVERY, None), P(None, EVERY)),
        check_vma=False,
    )
```

```python
import jax
import jax.numpy as jnp
from jax import lax
from jax.experimental import pallas as pl
from jax.experimental.pallas import tpu as pltpu
from jax.sharding import Mesh
from jax.sharding import PartitionSpec as P

CAP = 3
CHIPS = ("z", "y", "x")
LON = ("y", "x", "c")
EVERY = ("z", "y", "x", "c")
BF = jnp.bfloat16
F32 = jnp.float32
I32 = jnp.int32
NODES = 64
D = 512
SLOTS = 8
CHUNK = 384
BLOCK_ROWS = 80
TABLE = 384
N_CHIPS = 64
MSG = 1280


def dot(a, b):
    return jnp.dot(a, b, preferred_element_type=F32)


def dot_nt(a, b):
    return lax.dot_general(a, b, (((1,), (1,)), ((), ())), preferred_element_type=F32)


def dot_tn(a, b):
    return lax.dot_general(a, b, (((0,), (0,)), ((), ())), preferred_element_type=F32)


def iota(shape, dim):
    return lax.broadcasted_iota(I32, shape, dim)


def hot(mask):
    return jnp.where(mask, 1.0, 0.0).astype(BF)


def slope_of(value, sig):
    return sig * (1.0 + value * (1.0 - sig))


def column_of(small):
    rows = small.shape[0]
    count = rows * 8
    spread = dot(hot(iota((count, rows), 0) // 8 == iota((count, rows), 1)), small.astype(F32).astype(BF))
    keep = iota((count, 8), 0) % 8 == iota((count, 8), 1)
    return jnp.sum(jnp.where(keep, spread, 0.0), axis=1, keepdims=True)


def id_columns(ids_ref, core):
    ids = ids_ref[...].reshape(8, 8)
    half = ids >> 1
    chip = column_of(half & 63)
    slot = column_of(half >> 6)
    mine = jnp.where(column_of(ids & 1) == core.astype(F32), 1.0, 0.0)
    return chip, slot, mine


def row_of(column):
    count = column.shape[0]
    eye = iota((count, count), 0) == iota((count, count), 1)
    return jnp.sum(jnp.where(eye, column, 0.0), axis=0, keepdims=True)


def routes(at, chip, slot, mine):
    chip, slot = chip.astype(I32), slot.astype(I32)
    usual = (mine > 0.5) & (slot < 5)
    main = hot(at == jnp.where(usual, chip * SLOTS + slot, -1))
    tails = [
        hot(at == jnp.where(usual & (slot >> 1 == t), chip * SLOTS + 6 + (slot & 1), -1)) for t in range(3)
    ]
    return main, tails, jnp.where(usual, chip * SLOTS + 5, -1), (mine > 0.5) & (slot >= 5)


def pool_kernel(ids_ref, ids_other_ref, h_ref, h_other_ref, out_ref, info_ref):
    core = lax.axis_index("c")
    a = id_columns(ids_ref, core)
    b = id_columns(ids_other_ref, core)
    chip, slot, mine = (jnp.concatenate([u, v], 0) for u, v in zip(a, b))
    at = iota(info_ref.shape, 1)
    info_ref[...] = jnp.where(at == 0, chip, jnp.where(at == 1, slot, mine))
    rows = iota((N_CHIPS * SLOTS, 2 * NODES), 0)
    main, tails, count, extra = routes(rows, row_of(chip), row_of(slot), row_of(mine))
    which = hot(iota((2 * NODES, 128), 1) == slot.astype(I32))
    h = jnp.concatenate([h_ref[...], h_other_ref[...]], 0)
    tile = [h[:, 128 * k : 128 * (k + 1)] for k in range(4)]
    extra = jnp.where(extra, 1.0, 0.0)
    left = dot(jnp.broadcast_to(extra, (8, 2 * NODES)).astype(BF), h)
    left_count = jnp.sum(extra, axis=1, keepdims=True)
    sums = [
        dot(jnp.concatenate([main, tails[t]], 1), jnp.concatenate([tile[t], tile[3]], 0)) for t in range(3)
    ]
    sums[0] = sums[0] + dot(hot(rows == count), which)
    for k in range(4):
        here = rows == k * SLOTS + 5
        lane = iota(rows.shape, 1)
        sums[0] = sums[0] + jnp.where(here & (lane == 5), left_count, 0.0)
        sums[1] = sums[1] + jnp.where(here, left[0:1, 128 * k : 128 * (k + 1)], 0.0)
    for t in range(3):
        out_ref[:, 128 * t : 128 * (t + 1)] = sums[t].astype(BF)


def coarse_kernel(got_ref, out_ref):
    total = jnp.sum(got_ref[...].astype(F32), axis=0)
    row = iota((SLOTS, 128), 0)
    tail = jnp.zeros((SLOTS, 128), F32)
    for s in range(5):
        line = total[6 + s % 2 : 7 + s % 2, 128 * (s // 2) : 128 * (s // 2 + 1)]
        tail = jnp.where(row == s, jnp.broadcast_to(line, tail.shape), tail)
    counts = jnp.broadcast_to(total[5:6, 0:128], (SLOTS, 128))
    count = jnp.sum(jnp.where(row == iota((SLOTS, 128), 1), counts, 0.0), axis=1, keepdims=True)
    scale = jnp.where(count > 0.5, lax.rsqrt(jnp.maximum(count, 1.0)), 0.0)
    body, tail = total * scale, tail * scale
    parts = []
    for t in range(3):
        even = jnp.broadcast_to(tail[2 * t : 2 * t + 1, :], tail.shape)
        uneven = jnp.broadcast_to(tail[2 * t + 1 : 2 * t + 2, :], tail.shape)
        part = body[:, 128 * t : 128 * (t + 1)]
        parts.append(jnp.where(row < 6, part, jnp.where(row == 6, even, uneven)))
    packed = jnp.concatenate(parts, 1).astype(BF)
    out_ref[...] = jnp.broadcast_to(packed[None], out_ref.shape)


def select_kernel(info_ref, got_ref, _agg, _gs, wc, wd, wn, out_ref, wc_ref, wd_ref, wn_ref, sems):
    copies = [
        pltpu.make_async_copy(a, b, sems.at[i])
        for i, (a, b) in enumerate(((wc, wc_ref), (wd, wd_ref), (wn, wn_ref)))
    ]
    for copy in copies:
        copy.start()
    info = info_ref[...]
    lanes = iota((2 * NODES, N_CHIPS * SLOTS), 1)
    main, tails, _, extra = routes(lanes, info[:, 0:1], info[:, 1:2], info[:, 2:3])
    got = got_ref[...]
    tile = [got[:, 128 * t : 128 * (t + 1)] for t in range(3)]
    chosen = [dot(main, got), dot(jnp.concatenate(tails, 1), jnp.concatenate(tile, 0))]
    left = [got_ref[k * SLOTS : (k + 1) * SLOTS, 128:256].astype(F32)[5:6, :] for k in range(4)]
    chosen = jnp.concatenate(chosen, 1) + jnp.where(extra, jnp.concatenate(left, 1), 0.0)
    out_ref[...] = chosen.astype(BF)
    for copy in copies:
        copy.wait()


def pack_kernel(
    owner_ref, source_ref, target_ref, first_ref, second_ref, h_ref,
    own_ref, other_ref, far_ref, sent_other_ref, sent_far_ref, block_ref,
):
    odd = lax.axis_index("z") % 2 == 1
    first, second = first_ref[...], second_ref[...]
    above = jnp.where(odd, first, second)
    below = jnp.where(odd, second, first)
    block_ref[...] = jnp.concatenate([above, h_ref[...], below], 0)
    lon = lax.axis_index(LON)
    code_other = jnp.where(lax.axis_index("c") == 0, 1, 31)
    lists = (other_ref, far_ref)
    for ref in lists:
        ref[...] = jnp.full(ref.shape, -1, I32)
    ranks = [jnp.int32(0), jnp.int32(0)]
    for b in range(source_ref.shape[0]):
        side = (owner_ref[b] - lon) & 31
        source = source_ref[b : b + 1, :]
        target = target_ref[b : b + 1, :]
        own_ref[b : b + 1, :] = jnp.where(side == 0, target, -1)
        for k, code in enumerate((code_other, 32 - code_other)):
            here = side == code
            place = jnp.where(here, jnp.minimum(ranks[k], 6), 7)
            lists[k][pl.ds(place, 1), :] = source
            lists[k][pl.ds(place + 8, 1), :] = target
            ranks[k] = ranks[k] + here.astype(I32)
    for ref, sent in zip(lists, (sent_other_ref, sent_far_ref)):
        source, target = ref[0:8, :], ref[8:16, :]
        parts = [source, target >> 3, target & 7, jnp.zeros((8, 128), I32)]
        sent[...] = jnp.concatenate([p.astype(F32) for p in parts], 1).astype(BF)


def counted(sources, targets, grid_rows):
    at = iota((grid_rows, 128), 0)
    node = iota((NODES, 128), 0)
    hit = jnp.concatenate([hot(at == t) for t in targets], 1)
    come = jnp.concatenate([hot(node == s) for s in sources], 1)
    return dot_nt(come, hit)


def tally_kernel(source_ref, target_ref, other_ref, far_ref, ct_ref):
    grid_rows = ct_ref.shape[1]
    step = 4
    total = jnp.zeros((NODES, grid_rows), F32)
    for b in range(0, source_ref.shape[0], step):
        total = total + counted(
            [source_ref[i : i + 1, :] for i in range(b, b + step)],
            [target_ref[i : i + 1, :] for i in range(b, b + step)],
            grid_rows,
        )
    ct_ref[0:NODES, :] = total.astype(BF)
    for k, ref in enumerate((other_ref, far_ref)):
        ct_ref[(k + 1) * NODES : (k + 2) * NODES, :] = counted(
            [ref[i : i + 1, :] for i in range(CAP)],
            [ref[8 + i : 9 + i, :] for i in range(CAP)],
            grid_rows,
        ).astype(BF)


def gather_kernel(ct_ref, cot_ref, cot_other_ref, cot_far_ref, gs_ref):
    total = dot(ct_ref[NODES : 2 * NODES, :], cot_other_ref[...])
    total = total + dot(ct_ref[2 * NODES : 3 * NODES, :], cot_far_ref[...])
    gs_ref[...] = total + dot(ct_ref[0:NODES, :], cot_ref[...])


def shifted(value, side, core):
    wide = value.astype(F32)
    amount = 4 if side else D - 4
    moved = pltpu.roll(wide, amount, 1)
    lanes = iota(value.shape, 1)
    kept = ((lanes >> 2) & 1) == side
    picked = jnp.where(core == side, wide, moved)
    return jnp.where(kept, picked, 0.0).astype(BF)


def whole_table(refs):
    blocks = [ref[...] for ref in refs]
    return jnp.concatenate([*blocks, jnp.zeros((TABLE - 4 * BLOCK_ROWS, D), BF)], 0)


def chosen_rows(codes_ref, k):
    toward_left = jnp.where(lax.axis_index("c") == 0, -1, 1)
    code = column_of(codes_ref[...].reshape(48, 8)).astype(I32)
    node = iota((6 * NODES, 1), 0) % NODES
    down = (code * 11) >> 5
    row = node // 8 + down
    col = node % 8 + code - 3 * down - 1
    step = jnp.where(col < 0, toward_left, jnp.where(col > 7, -toward_left, 0))
    place = (1 + k + step) * BLOCK_ROWS + row * 8 + (col & 7)
    return hot(iota((6 * NODES, TABLE), 1) == place)


def edges_kernel(
    codes_ref, codes_other_ref, far_ref, own_ref, other_ref, other_far_ref, ws_ref, wt_ref,
    slope_ref, agg_ref, table_side_ref, h_side_ref, agg_side_ref,
):
    core = lax.axis_index("c")
    table = whole_table((far_ref, own_ref, other_ref, other_far_ref))
    table_side_ref[...] = shifted(table, 0, core)
    for k, (codes, own) in enumerate(((codes_ref, own_ref), (codes_other_ref, other_ref))):
        beside = dot(chosen_rows(codes, k), table).astype(BF)
        toward = dot(own[8:72, :], wt_ref[...])
        pre = dot(beside, ws_ref[...])
        agg = jnp.zeros((NODES, D), F32)
        for s in range(6):
            value = pre[s * NODES : (s + 1) * NODES, :] + toward
            sig = jax.nn.sigmoid(value)
            agg = agg + value * sig
            at = (k * 6 + s) * NODES
            slope_ref[at : at + NODES, :] = slope_of(value, sig).astype(BF)
        agg = agg.astype(BF)
        rows = pl.ds(k * NODES, NODES)
        agg_ref[rows, :] = agg
        agg_side_ref[rows, :] = shifted(agg, 0, core)
        h_side_ref[rows, :] = shifted(own[8:72, :], 1, core)


def main_kernel(
    cin_ref, cin_other_ref, codes_ref, codes_other_ref, own_ref, other_ref,
    slope_ref, agg_ref, table_side_ref, h_side_ref, agg_side_ref, gs_ref, gs_other_ref, wc_ref, wd_ref, wn_ref, sent_far_ref,
    mesh_ref, message_ref, to_far_ref, room,
):
    def leave(lanes, value):
        room[:, lanes] = value.astype(BF)

    core = lax.axis_index("c")
    chosen = jnp.concatenate([chosen_rows(codes_ref, 0), chosen_rows(codes_other_ref, 1)], 0)
    cin = jnp.concatenate(
        [
            cin_ref[:NODES, :].astype(F32) + cin_other_ref[NODES:, :].astype(F32),
            cin_ref[NODES:, :].astype(F32) + cin_other_ref[:NODES, :].astype(F32),
        ],
        0,
    ).astype(BF)
    h = jnp.concatenate([own_ref[8:72, :], other_ref[8:72, :]], 0)
    cpre = dot(cin, wc_ref[...])
    csig = jax.nn.sigmoid(cpre)
    npre = dot(agg_ref[...], wn_ref[...]) + (cpre * csig).astype(BF).astype(F32)
    nsig = jax.nn.sigmoid(npre)
    mesh_out = (h.astype(F32) + npre * nsig).astype(BF)
    mesh_ref[...] = mesh_out[:NODES, :]
    pre = dot(mesh_out, wd_ref[...])
    sig = jax.nn.sigmoid(pre)
    message = (pre * sig).astype(BF)
    message_ref[...] = message
    to_far_ref[...] = jnp.concatenate([message[:NODES, :], sent_far_ref[...]], 0)
    gs = jnp.concatenate([gs_ref[...], gs_other_ref[...]], 0)
    d_source = (gs * slope_of(pre, sig)).astype(BF)
    d_out = dot_nt(d_source, wd_ref[...])
    d_node = (d_out * slope_of(npre, nsig)).astype(BF)
    leave(
        pl.ds(2 * D, D // 2),
        dot_tn(
            jnp.concatenate([shifted(mesh_out, 0, core), shifted(mesh_out, 1, core)], 0),
            jnp.concatenate([d_source[:, : D // 2], d_source[:, D // 2 :]], 0),
        ),
    )
    d_agg = dot_nt(d_node, wn_ref[...])
    d_coarse = (d_node.astype(F32) * slope_of(cpre, csig)).astype(BF)
    leave(
        pl.ds(D, D),
        dot_tn(
            jnp.concatenate([agg_side_ref[...], shifted(cin, 1, core)], 0),
            jnp.concatenate([d_node, d_coarse], 0),
        ),
    )
    d_edges, sums = [], []
    for k in range(2):
        part = d_agg[k * NODES : (k + 1) * NODES, :]
        d_sum = jnp.zeros((NODES, D), F32)
        for s in range(6):
            at = (k * 6 + s) * NODES
            d_edge = (part * slope_ref[at : at + NODES, :].astype(F32)).astype(BF)
            d_sum = d_sum + d_edge.astype(F32)
            d_edges.append(d_edge)
        sums.append(d_sum.astype(BF))
    scattered = dot_tn(chosen, jnp.concatenate(d_edges, 0)).astype(BF)
    leave(
        pl.ds(0, D),
        dot_tn(
            jnp.concatenate([table_side_ref[...], h_side_ref[...]], 0),
            jnp.concatenate([scattered, *sums], 0),
        ),
    )


def grid_kernel(ct_ref, message_ref, lists_ref, far_ref, out_ref, done_ref):
    done_ref[...] = jnp.zeros(done_ref.shape, F32)
    grid_rows = out_ref.shape[0]
    tables = [ct_ref[0:NODES, :]]
    for lists in (lists_ref[...], far_ref[NODES : NODES + 8, :]):
        lists = lists.astype(F32)
        source = lists[:, 0:128].astype(I32)
        target = (lists[:, 128:256] * 8.0 + lists[:, 256:384]).astype(I32)
        tables.append(
            counted(
                [source[i : i + 1, :] for i in range(CAP)],
                [target[i : i + 1, :] for i in range(CAP)],
                grid_rows,
            ).astype(BF)
        )
    rows = jnp.concatenate([message_ref[...], far_ref[0:NODES, :]], 0)
    out_ref[...] = dot_tn(jnp.concatenate(tables, 0), rows).astype(BF)


def sum_kernel(got_ref, share_ref, square_ref):
    total = jnp.sum(got_ref[...].astype(F32), axis=0)
    share_ref[...] = total
    square = jnp.sum(jnp.sum(total * total, axis=0, keepdims=True), axis=1, keepdims=True)
    square_ref[...] = jnp.broadcast_to(square, square_ref.shape)


def clip_kernel(squares_ref, share_ref, _done, out_ref):
    total = jnp.sum(squares_ref[...], axis=0, keepdims=True)
    norm = jnp.sqrt(jnp.max(total, axis=1, keepdims=True)) + 1e-06
    value = share_ref[...] / norm
    for m in range(5):
        for r in range(4):
            if m < 4:
                row = (m % 2) * 4 + r
                line = value[row : row + 1, (m // 2) * D : (m // 2 + 1) * D]
            else:
                line = jnp.concatenate(
                    [value[r : r + 1, 2 * D :], value[r + 4 : r + 5, 2 * D :]], 1
                )
            out_ref[m : m + 1, r * D : (r + 1) * D] = line


class Fetched:
    def __init__(self, ref, room, sem):
        self.copy, self.room, self.waited = pltpu.make_async_copy(ref, room, sem), room, False
        self.shape, self.dtype = room.shape, room.dtype
        self.copy.start()

    def __getitem__(self, at):
        if not self.waited:
            self.copy.wait()
            self.waited = True
        return self.room[at]


def call(kernel, outs, *args, smem=(), hbm=(), raw=(), last=(), raw_out=(), scratch=()):
    space = [
        pltpu.SMEM if i in smem else pltpu.HBM if i in hbm or i in raw else pltpu.VMEM
        for i in range(len(args))
    ]
    shapes = [
        pltpu.HBM(s, d) if i in raw_out else jax.ShapeDtypeStruct(s, d) if i in last else pltpu.VMEM(s, d)
        for i, (s, d) in enumerate(outs)
    ]
    args = [
        a if i in smem else pltpu.with_memory_space_constraint(a, space[i])
        for i, a in enumerate(args)
    ]
    ends = len(args) + len(outs)

    def whole(*refs):
        refs = list(refs)
        own, rooms, sems = refs[ends : ends + len(scratch)], refs[ends + len(scratch) : -1], refs[-1]
        for k, i in enumerate(hbm):
            refs[i] = Fetched(refs[i], rooms[k], sems.at[k])
        kernel(*refs[:ends], *own)

    out = pl.pallas_call(
        whole if hbm else kernel,
        out_shape=shapes,
        in_specs=[pl.BlockSpec(memory_space=m) for m in space],
        out_specs=[
            pl.BlockSpec(memory_space=pltpu.HBM if i in raw_out else pltpu.VMEM) for i in range(len(outs))
        ],
        scratch_shapes=[
            *scratch,
            *(
                [
                    *(pltpu.VMEM(args[i].shape, args[i].dtype) for i in hbm),
                    pltpu.SemaphoreType.DMA((len(hbm),)),
                ]
                if hbm
                else ()
            ),
        ],
        compiler_params=pltpu.CompilerParams(vmem_limit_bytes=24 << 20),
    )(*args)
    return out if len(outs) > 1 else out[0]


def local(
    mesh_latent, grid_cotangent, w_source, w_target, w_node, w_coarse, w_decode,
    neighbour_codes, coarse_ids, edge_source, edge_target, edge_owner,
):
    height, breadth, width = mesh_latent.shape
    nodes = height * breadth
    grid_rows = grid_cotangent.shape[0]
    blocks = edge_owner.shape[0]
    core_pairs = [(0, 1), (1, 0)]
    chip_pairs = [(i, (i + 1) % 32) for i in range(1, 32, 2)]
    chip_pairs += [(b, a) for a, b in chip_pairs]
    done_shape = ((8, 128), F32)

    def other(value):
        return lax.ppermute(value, "c", core_pairs)

    def far(value):
        return lax.ppermute(value, LON, chip_pairs)

    def swapped(value, axes=CHIPS):
        return lax.all_to_all(value, axes, split_axis=0, concat_axis=0, tiled=True)

    h = mesh_latent.reshape(nodes, width)
    ids = jnp.transpose(coarse_ids, (0, 2, 1))
    ids_other = other(ids)
    h_other = other(h)
    odd = lax.axis_index("z") % 2 == 1
    top, bottom = mesh_latent[0], mesh_latent[height - 1]
    first = lax.ppermute(jnp.where(odd, top, bottom), "z", [(0, 1), (1, 0), (2, 3), (3, 2)])
    second = lax.ppermute(jnp.where(odd, bottom, top), "z", [(1, 2), (2, 1)])
    pooled, info = call(
        pool_kernel, [((N_CHIPS * SLOTS, CHUNK), BF), ((2 * NODES, 128), F32)],
        ids, ids_other, h, h_other, hbm=(0, 2), last=(0,),
    )
    pooled = swapped(pooled.reshape(N_CHIPS, SLOTS, CHUNK))

    source = edge_source.reshape(blocks, -1)
    target = edge_target.reshape(blocks, -1)
    lists = ((16, 128), I32)
    own_target, list_other, list_far, sent_other, sent_far, block = call(
        pack_kernel,
        [
            ((blocks, 128), I32), lists, lists, ((8, D), BF), ((8, D), BF), ((BLOCK_ROWS, D), BF),
        ],
        edge_owner.reshape(blocks), source, target, first, second, h, smem=(0,), hbm=(1, 2, 5),
    )
    cot_far = far(grid_cotangent)
    block_far = far(block)
    cot_other = other(grid_cotangent)
    block_other = other(block)
    codes_other = other(neighbour_codes)
    lists_other = other(sent_other)
    ct = call(
        tally_kernel, [((3 * NODES, grid_rows), BF)],
        source, own_target, list_other, list_far, hbm=(0,),
    )
    coarse = call(coarse_kernel, [((N_CHIPS, SLOTS, CHUNK), BF)], pooled, last=(0,))
    coarse = swapped(coarse).reshape(N_CHIPS * SLOTS, CHUNK)

    gs = call(
        gather_kernel, [((NODES, D), F32)], ct, grid_cotangent, cot_other, cot_far, hbm=(1,)
    )
    block_other_far = other(block_far)
    gs_pair = other(gs)
    around = (block_far, block, block_other, block_other_far)
    pair = ((2 * NODES, D), BF)
    slopes, agg, *sides = call(
        edges_kernel,
        [((12 * NODES, D), BF), pair, ((TABLE, D), BF), pair, pair],
        neighbour_codes, codes_other, *around, w_source, w_target, hbm=(0, 6, 7),
    )
    weight = (w_coarse.shape, BF)
    cin, wc, wd, wn = call(
        select_kernel, [pair, weight, weight, weight],
        info, coarse, agg, gs_pair, w_coarse, w_decode, w_node,
        raw=(4, 5, 6), scratch=(pltpu.SemaphoreType.DMA((3,)),),
    )
    cin_other = other(cin)
    sent = ((NODES + 8, D), BF)
    mesh_out, message, to_far, msg = call(
        main_kernel,
        [((NODES, D), BF), ((2 * NODES, D), BF), sent, ((N_CHIPS * 8, MSG), BF)],
        cin, cin_other, neighbour_codes, codes_other, block, block_other, slopes, agg, *sides, gs, gs_pair,
        wc, wd, wn, sent_far,
        hbm=(2,), last=(0, 3),
    )
    arrived = swapped(msg.reshape(N_CHIPS, 8, MSG))
    got_far = far(to_far)
    share, square = call(sum_kernel, [((8, MSG), F32), ((128, 128), F32)], arrived)
    squares = swapped(square.reshape(128, 1, 128), EVERY).reshape(128, 128)
    grid_out, placed = call(
        grid_kernel, [((grid_rows, D), BF), done_shape], ct, message, lists_other, got_far, last=(0,),
    )
    clipped = call(clip_kernel, [((5, 4 * D), F32)], squares, share, placed, last=(0,))
    return mesh_out.reshape(height, breadth, width), grid_out, clipped


def solution(mesh):
    split = Mesh(mesh.devices.reshape(4, 4, 4, 2), EVERY)
    return jax.shard_map(
        local,
        mesh=split,
        in_specs=(
            P("z", LON, None),
            P(EVERY, None),
            P(),
            P(),
            P(),
            P(),
            P(),
            P(None, "z", LON),
            P("z", LON, None),
            P(EVERY),
            P(EVERY),
            P(EVERY, None),
        ),
        out_specs=(P("z", LON, None), P(EVERY, None), P(None, EVERY)),
        check_vma=False,
    )
```
